32 devices in a mesh: parts: 1, tile: 16 (over z, y, core), face: 2 (over x), sub: 1.
Axes of the slice: x: 2, y: 2, z: 4, core: 2. Of those that a mesh axis runs over, the one named last changes fastest.
Arguments:
- fields: bfloat16 [96, 4, 32, 96], P('sub', 'face', 'tile', 'parts'), may hold values from -6 to 6
- upstream: bfloat16 [96, 4, 32, 96], P('sub', 'face', 'tile', 'parts'), may hold values from -6 to 6
- kernel_one: bfloat16 [3, 3, 96, 96], replicated, may hold values from -0.21875 to 0.21875
- kernel_two: bfloat16 [3, 3, 96, 96], replicated, may hold values from -0.21875 to 0.21875
Outputs:
- result: bfloat16 [96, 4, 32, 96], P('sub', 'face', 'tile', 'parts')
- fields_grad: bfloat16 [96, 4, 32, 96], P('sub', 'face', 'tile', 'parts')
- kernel_one_grad: float32 [3, 3, 96, 96], P('parts', None, None, 'sub')
- kernel_two_grad: float32 [3, 3, 96, 96], P('parts', None, None, 'sub')
The draws below stay inside these ranges and needn't reach their ends.
All inputs are finite; a program needn't handle non-finite values.
Results may differ from the reference program's by a relative error of at most 0.0049.
Values may be sent and summed in bfloat16 or wider, within the bound.
A program may use at most 128 MiB of HBM per device.

```python
import jax
import jax.numpy as jnp
from jax import lax

C = 96
SIDE = 32


def level_of(key, shape, shards, smallest, largest):
    def one(dim, shards_of):
        steps = jax.random.uniform(jax.random.fold_in(jax.random.fold_in(key, 6), dim), (shards_of,), jnp.float32, smallest / len(shards), largest / len(shards))
        return jnp.repeat(jnp.exp(steps), shape[dim] // shards_of).reshape((-1,) + (1,) * (len(shape) - dim - 1))

    gain = one(*shards[0])
    for cut in shards[1:]:
        gain = gain * one(*cut)
    return gain


def scatter_about(own_key, dims, scale, reach, shards=(), kind=jnp.bfloat16):
    entries = jax.random.normal(own_key, dims, jnp.float32) * scale
    if len(shards) > 0:
        entries = level_of(own_key, dims, shards, -0.22, 0.18) * entries
    return jnp.clip(entries, min=-reach, max=reach).astype(kind)


def setup_inputs(seed: int = 0, part: int = 0) -> dict:
    key_list = jax.random.split(jax.random.key(seed), 5)
    own_keys = jax.random.split(jax.random.fold_in(key_list[4], part), 5)
    fields = scatter_about(own_keys[0], (C, 4, SIDE, 3 * SIDE), 1.0, 6.0, ((1, 2), (2, 16)))
    upstream = scatter_about(own_keys[1], (C, 4, SIDE, 3 * SIDE), 1.0, 6.0, ((1, 2), (2, 16)))
    kernel_one = scatter_about(key_list[2], (3, 3, C, C), (9 * C) ** -0.5, 0.21875)
    kernel_two = scatter_about(key_list[3], (3, 3, C, C), (9 * C) ** -0.5, 0.21875)
    return {"fields": fields, "upstream": upstream, "kernel_one": kernel_one, "kernel_two": kernel_two}


def activate(values):
    return jax.nn.gelu(values, approximate=True)

def sphere_pad(field):
    side = field.shape[2]
    before = jnp.roll(field, 1, axis=1)
    after = jnp.roll(field, -1, axis=1)
    top_line = after[:, :, 0, 0:side]
    bottom_line = before[:, :, side - 1, 2 * side:3 * side]
    left_line = jnp.concatenate([before[:, :, 0:side, 0], before[:, :, side - 1, 0:2 * side]], axis=2)
    right_line = jnp.concatenate([after[:, :, 0, side:3 * side], after[:, :, 0:side, 3 * side - 1]], axis=2)
    corner = jnp.zeros(field.shape[0:2] + (1,), field.dtype)
    top_row = jnp.concatenate([corner, top_line, corner], axis=2)
    bottom_row = jnp.concatenate([corner, bottom_line, corner], axis=2)
    middle = jnp.concatenate([left_line[:, :, None, :], field, right_line[:, :, None, :]], axis=2)
    return jnp.concatenate([top_row[:, :, :, None], middle, bottom_row[:, :, :, None]], axis=3)

def sphere_fold(gradient):
    side = gradient.shape[2] - 2
    height = 3 * side
    interior = gradient[:, :, 1:side + 1, 1:height + 1]
    grad_top = gradient[:, :, 1:side + 1, 0]
    grad_bottom = gradient[:, :, 1:side + 1, height + 1]
    grad_left = gradient[:, :, 0, 1:height + 1]
    grad_right = gradient[:, :, side + 1, 1:height + 1]
    to_after = jnp.zeros_like(interior)
    to_after = to_after.at[:, :, 0, 0:side].add(grad_top)
    to_after = to_after.at[:, :, 0, side:height].add(grad_right[:, :, 0:2 * side])
    to_after = to_after.at[:, :, 0:side, height - 1].add(grad_right[:, :, 2 * side:height])
    to_before = jnp.zeros_like(interior)
    to_before = to_before.at[:, :, side - 1, 2 * side:height].add(grad_bottom)
    to_before = to_before.at[:, :, 0:side, 0].add(grad_left[:, :, 0:side])
    to_before = to_before.at[:, :, side - 1, 0:2 * side].add(grad_left[:, :, side:height])
    return interior + jnp.roll(to_after, 1, axis=1) + jnp.roll(to_before, -1, axis=1)

def convolve(padded, kernel):
    return lax.conv_general_dilated(padded.astype(jnp.float32), kernel.astype(jnp.float32), (1, 1), 'VALID', dimension_numbers=('CNHW', 'HWIO', 'CNHW'), precision=lax.Precision.HIGHEST, preferred_element_type=jnp.float32)

def spread(cotangent, kernel):
    flipped = jnp.flip(kernel, (0, 1)).transpose(0, 1, 3, 2)
    return lax.conv_general_dilated(cotangent.astype(jnp.float32), flipped.astype(jnp.float32), (1, 1), ((2, 2), (2, 2)), dimension_numbers=('CNHW', 'HWIO', 'CNHW'), precision=lax.Precision.HIGHEST, preferred_element_type=jnp.float32)

def weight_terms(padded, cotangent):
    columns = cotangent.shape[2]
    height = cotangent.shape[3]
    flat_cot = cotangent.astype(jnp.float32).reshape(cotangent.shape[0], -1)
    tap_rows = []
    for col_tap in range(3):
        row_list = []
        for row_tap in range(3):
            tap_cells = padded[:, :, col_tap:col_tap + columns, row_tap:row_tap + height]
            tap_cells = tap_cells.astype(jnp.float32).reshape(padded.shape[0], -1)
            row_list.append(lax.dot_general(tap_cells, flat_cot, (((1,), (1,)), ((), ())), precision=lax.Precision.HIGHEST, preferred_element_type=jnp.float32))
        tap_rows.append(jnp.stack(row_list))
    return jnp.stack(tap_rows)

def reference(fields, upstream, kernel_one, kernel_two):
    face_side = fields.shape[2]
    cell_scale = 1.0 / (face_side * jnp.sqrt(jnp.float32(12.0)))
    padded_one = sphere_pad(fields)
    pre_one = convolve(padded_one, kernel_one)
    hidden = activate(pre_one).astype(jnp.bfloat16)
    padded_two = sphere_pad(hidden)
    result = convolve(padded_two, kernel_two).astype(jnp.bfloat16)
    hidden_grad = sphere_fold(spread(upstream, kernel_two))
    unused, pullback = jax.vjp(activate, pre_one)
    pre_grad = pullback(hidden_grad)[0].astype(jnp.bfloat16)
    fields_grad = sphere_fold(spread(pre_grad, kernel_one)).astype(jnp.bfloat16)
    kernel_one_grad = weight_terms(padded_one, pre_grad) * cell_scale
    kernel_two_grad = weight_terms(padded_two, upstream) * cell_scale
    return (result, fields_grad, kernel_one_grad, kernel_two_grad)
```

```python
import functools

import jax
import jax.numpy as jnp
from jax import lax
from jax.experimental import pallas as pl
from jax.experimental.pallas import tpu as pltpu
from jax.sharding import PartitionSpec as P

MESH = pl.DeviceIdType.MESH
F32 = jnp.float32
BF16 = jnp.bfloat16


def gelu_parts(v):
    root = 0.7978845608028654
    cube = 0.044715 * (v * v * v)
    th = jnp.tanh(root * (v + cube))
    value = v * (0.5 * (1.0 + th))
    slope = 0.5 * (1.0 + th) + 0.5 * v * (1.0 - th * th) * root * (1.0 + 0.134145 * (v * v))
    return value, slope


def product(a, b, da, db):
    return lax.dot_general(a, b, (((da,), (db,)), ((), ())), preferred_element_type=F32)


def body(n_t, n_f, scale, x, k1, k2, res_o, fg_o, w1_o, w2_o,
         y, rows, lh, rh, ap, bm, tr, dr, tl, dl, pad, xb, xf1, xf2,
         acc, sbuf, rbuf, obuf,
         col_s, col_r, a_s, a_r, b_s, b_r, t_s, t_r, d_s, d_r, w_s, w_r):
    _, G, J, H, C = x.shape
    S = H // 3
    W = S + 16
    M = G * J * H
    t = lax.axis_index("tile")
    f = lax.axis_index("face")
    fn = lax.rem(f + 1, n_f)
    fp = lax.rem(f + n_f - 1, n_f)
    first = t == 0
    last = t == n_t - 1

    def where_to(tile, face):
        return {"tile": tile, "face": face}

    def remote(src, dst, s, r, dev):
        return pltpu.make_async_remote_copy(
            src_ref=src, dst_ref=dst, send_sem=s, recv_sem=r, device_id=dev, device_id_type=MESH)

    def stage_rows(p, src):
        for u in range(2):
            for q in range(G):
                for j in range(J):
                    v = src[u, q, j].astype(F32)
                    rows[p, 0, u, q, j:j + 1, :] = v[0:1]
                    rows[p, 1, u, q, j:j + 1, :] = v[H - 1:H]

    def copies(p, src):
        c0, cl = src.at[:, :, 0], src.at[:, :, J - 1]
        right = lambda: remote(cl, lh.at[p], col_s.at[p, 0], col_r.at[p, 0], where_to(jnp.minimum(t + 1, n_t - 1), f))
        left = lambda: remote(c0, rh.at[p], col_s.at[p, 1], col_r.at[p, 1], where_to(jnp.maximum(t - 1, 0), f))
        seam = []
        if G > 1:
            seam.append((first, lambda: remote(src.at[:, 1:G, 0], rh.at[p, :, 0:G - 1], col_s.at[p, 2], col_r.at[p, 2], where_to(n_t - 1, f))))
            seam.append((last, lambda: remote(src.at[:, 0:G - 1, J - 1], lh.at[p, :, 1:G], col_s.at[p, 3], col_r.at[p, 3], where_to(0, f))))
        seam.append((first, lambda: remote(src.at[:, 0:1, 0], rh.at[p, :, G - 1:G], col_s.at[p, 4], col_r.at[p, 4], where_to(n_t - 1, fp))))
        seam.append((last, lambda: remote(src.at[:, G - 1:G, J - 1], lh.at[p, :, 0:1], col_s.at[p, 5], col_r.at[p, 5], where_to(0, fn))))
        a_own = lambda d: remote(src.at[:, 1:G, 0, 0:W], ap.at[p, :, 0:G - 1], a_s.at[p, 0, d], a_r.at[p, 0], where_to(d, f))
        a_oth = lambda d: remote(src.at[:, 0:1, 0, 0:W], ap.at[p, :, G - 1:G], a_s.at[p, 1, d], a_r.at[p, 1], where_to(d, fp))
        b_own = lambda d: remote(src.at[:, 0:G - 1, J - 1, H - W:H], bm.at[p, :, 1:G], b_s.at[p, 0, d], b_r.at[p, 0], where_to(d, f))
        b_oth = lambda d: remote(src.at[:, G - 1:G, J - 1, H - W:H], bm.at[p, :, 0:1], b_s.at[p, 1, d], b_r.at[p, 1], where_to(d, fn))
        t_own = lambda d: remote(rows.at[p, 0, :, 0:G - 1], tr.at[p, d, :, 1:G], t_s.at[p, 0], t_r.at[p, 0, d], where_to(0, f))
        t_oth = lambda d: remote(rows.at[p, 0, :, G - 1:G], tr.at[p, d, :, 0:1], t_s.at[p, 1], t_r.at[p, 1, d], where_to(0, fn))
        d_own = lambda d: remote(rows.at[p, 1, :, 1:G], dr.at[p, d, :, 0:G - 1], d_s.at[p, 0], d_r.at[p, 0, d], where_to(n_t - 1, f))
        d_oth = lambda d: remote(rows.at[p, 1, :, 0:1], dr.at[p, d, :, G - 1:G], d_s.at[p, 1], d_r.at[p, 1, d], where_to(n_t - 1, fp))
        return right, left, seam, a_own, a_oth, b_own, b_oth, t_own, t_oth, d_own, d_oth

    def start(p, src):
        right, left, seam, a_own, a_oth, b_own, b_oth, t_own, t_oth, d_own, d_oth = copies(p, src)

        @pl.when(jnp.logical_not(last))
        def _():
            right().start()

        @pl.when(jnp.logical_not(first))
        def _():
            left().start()

        for cond, make in seam:
            @pl.when(cond)
            def _(make=make):
                make().start()

        t_oth(t).start()
        d_oth(t).start()

        @pl.when(first)
        def _():
            if G > 1:
                @pl.loop(1, n_t)
                def _(d):
                    a_own(d).start()
                ap[p, :, 0:G - 1] = src[:, 1:G, 0, 0:W]
                tr[p, 0, :, 1:G] = rows[p, 0, :, 0:G - 1]

            @pl.loop(0, n_t)
            def _(d):
                a_oth(d).start()

        @pl.when(last)
        def _():
            if G > 1:
                @pl.loop(0, n_t - 1)
                def _(d):
                    b_own(d).start()
                bm[p, :, 1:G] = src[:, 0:G - 1, J - 1, H - W:H]
                dr[p, n_t - 1, :, 0:G - 1] = rows[p, 1, :, 1:G]

            @pl.loop(0, n_t)
            def _(d):
                b_oth(d).start()

        if G > 1:
            @pl.when(jnp.logical_not(first))
            def _():
                t_own(t).start()

            @pl.when(jnp.logical_not(last))
            def _():
                d_own(t).start()

    def await_arrivals(p, src):
        right, left, seam, a_own, a_oth, b_own, b_oth, t_own, t_oth, d_own, d_oth = copies(p, src)

        @pl.when(jnp.logical_not(first))
        def _():
            right().wait_recv()
            if G > 1:
                a_own(0).wait_recv()

        @pl.when(jnp.logical_not(last))
        def _():
            left().wait_recv()
            if G > 1:
                b_own(0).wait_recv()

        for cond, make in seam:
            other = last if cond is first else first

            @pl.when(other)
            def _(make=make):
                make().wait_recv()

        a_oth(0).wait_recv()
        b_oth(0).wait_recv()

        @pl.when(first)
        def _():
            if G > 1:
                @pl.loop(1, n_t)
                def _(d):
                    t_own(d).wait_recv()

            @pl.loop(0, n_t)
            def _(d):
                t_oth(d).wait_recv()
            for d in range(n_t):
                tl[:, :, 8 + d * J:8 + (d + 1) * J, :] = tr[p, d]

        @pl.when(last)
        def _():
            if G > 1:
                @pl.loop(0, n_t - 1)
                def _(d):
                    d_own(d).wait_recv()

            @pl.loop(0, n_t)
            def _(d):
                d_oth(d).wait_recv()
            for d in range(n_t):
                dl[:, :, 8 + d * J:8 + (d + 1) * J, :] = dr[p, d]

    def await_sends(p, src):
        right, left, seam, a_own, a_oth, b_own, b_oth, t_own, t_oth, d_own, d_oth = copies(p, src)

        @pl.when(jnp.logical_not(last))
        def _():
            right().wait_send()
            if G > 1:
                d_own(t).wait_send()

        @pl.when(jnp.logical_not(first))
        def _():
            left().wait_send()
            if G > 1:
                t_own(t).wait_send()

        for cond, make in seam:
            @pl.when(cond)
            def _(make=make):
                make().wait_send()
        t_oth(t).wait_send()
        d_oth(t).wait_send()

        @pl.when(first)
        def _():
            if G > 1:
                @pl.loop(1, n_t)
                def _(d):
                    a_own(d).wait_send()

            @pl.loop(0, n_t)
            def _(d):
                a_oth(d).wait_send()

        @pl.when(last)
        def _():
            if G > 1:
                @pl.loop(0, n_t - 1)
                def _(d):
                    b_own(d).wait_send()

            @pl.loop(0, n_t)
            def _(d):
                b_oth(d).wait_send()

    spot = lax.broadcasted_iota(jnp.int32, (8, W), 0) + (t * J - 1)
    lane = lax.broadcasted_iota(jnp.int32, (8, W), 1)
    spread_a = spot == lane
    spread_b = spot + 16 == lane

    def one_hot(mask):
        return jnp.where(mask, 1.0, 0.0).astype(BF16)

    def fill_columns(u, src):
        for q in range(G):
            for j in range(J):
                pad[q, 1 + j, 8:8 + H, :] = src[u, q, j].astype(F32)

    def forward_taps(p, src, out):
        fill_columns(0, src)
        for q in range(G):
            @pl.when(jnp.logical_not(first))
            def _():
                pad[q, 0, 8:8 + H, :] = lh[p, 0, q].astype(F32)

            @pl.when(first)
            def _():
                pad[q, 0, 8:8 + S, :] = tl[0, q, 8:8 + S, :]
                pad[q, 0, 8 + S:8 + H, :] = lh[p, 0, q, 0:2 * S].astype(F32)

            @pl.when(jnp.logical_not(last))
            def _():
                pad[q, J + 1, 8:8 + H, :] = rh[p, 0, q].astype(F32)

            @pl.when(last)
            def _():
                pad[q, J + 1, 8:8 + 2 * S, :] = rh[p, 0, q, S:H].astype(F32)
                pad[q, J + 1, 8 + 2 * S:8 + H, :] = dl[0, q, 8:8 + S, :]
            top = product(one_hot(spread_a & (lane < S)), ap[p, 0, q], 1, 0)
            low = product(one_hot(spread_b & (lane >= 16)), bm[p, 0, q], 1, 0)
            for j in range(J + 2):
                pad[q, j, 7:8, :] = top[j:j + 1]
                pad[q, j, 8 + H:9 + H, :] = low[j:j + 1]
        for a in range(3):
            for b in range(3):
                for q in range(G):
                    for j in range(J):
                        m = (q * J + j) * H
                        out[3 * a + b, m:m + H, :] = pad[q, j + a, 7 + b:7 + b + H, :].astype(BF16)

    def backward_taps(p, src, out):
        fill_columns(1, src)
        for q in range(G):
            @pl.when(jnp.logical_not(first))
            def _():
                pad[q, 0, 8:8 + H, :] = lh[p, 1, q].astype(F32)

            @pl.when(first)
            def _():
                pad[q, 0, :, :] = jnp.zeros((H + 16, C), F32)

            @pl.when(jnp.logical_not(last))
            def _():
                pad[q, J + 1, 8:8 + H, :] = rh[p, 1, q].astype(F32)

            @pl.when(last)
            def _():
                pad[q, J + 1, :, :] = jnp.zeros((H + 16, C), F32)
            for j in range(J + 2):
                pad[q, j, 7:8, :] = jnp.zeros((1, C), F32)
                pad[q, j, 8 + H:9 + H, :] = jnp.zeros((1, C), F32)
        for a in range(3):
            for b in range(3):
                for q in range(G):
                    for j in range(J):
                        m = (q * J + j) * H
                        out[3 * a + b, m:m + H, :] = pad[q, j - a + 2, 9 - b:9 - b + H, :]
        for q in range(G):
            top = product(one_hot(spread_a), ap[p, 1, q], 1, 0)
            low = product(one_hot(spread_b), bm[p, 1, q], 1, 0)
            for b in range(3):
                for j in range(J):
                    m = (q * J + j) * H
                    out[b, m:m + 1, :] += top[j + 2 - b:j + 3 - b]
                    out[6 + b, m + H - 1:m + H, :] += low[j + 2 - b:j + 3 - b]

        @pl.when(last)
        def _():
            for q in range(G):
                m = (q * J + J - 1) * H
                pad[q, J + 1, 8:8 + H, :] = rh[p, 1, q].astype(F32)
                for e in range(3):
                    out[e, m:m + 2 * S, :] += pad[q, J + 1, 8 + S + 1 - e:8 + H + 1 - e, :]
                    out[3 * e + 2, m + 2 * S:m + H, :] += dl[1, q, 9 - e:9 - e + S, :]

        @pl.when(first)
        def _():
            for q in range(G):
                m = q * J * H
                pad[q, 0, 8:8 + H, :] = lh[p, 1, q].astype(F32)
                for e in range(3):
                    out[3 * e, m:m + S, :] += tl[1, q, 9 - e:9 - e + S, :]
                    pass
                for e in range(3):
                    out[6 + e, m + S:m + H, :] += pad[q, 0, 9 - e:9 - e + 2 * S, :]

    def apply(taps, k, dim):
        total = product(taps[0].astype(BF16), k[0, 0], 1, dim)
        for n in range(1, 9):
            total = total + product(taps[n].astype(BF16), k[n // 3, n % 3], 1, dim)
        return total

    def flat(src, u):
        return jnp.concatenate([src[u, q, j] for q in range(G) for j in range(J)], axis=0)

    per = C // 16

    def weight_terms(taps, cot, base):
        for n in range(9):
            term = product(taps[n], cot, 0, 0) * scale
            acc[base + n * per:base + (n + 1) * per] = term.reshape(per, 16, C)

    barrier = pltpu.get_barrier_semaphore()

    @pl.loop(0, n_f)
    def _(df):
        @pl.loop(0, n_t)
        def _(dt):
            @pl.when(jnp.logical_or(df != f, dt != t))
            def _():
                pl.semaphore_signal(barrier, inc=1, device_id=where_to(dt, df), device_id_type=MESH)
    stage_rows(0, x)
    tl[...] = jnp.zeros_like(tl)
    dl[...] = jnp.zeros_like(dl)
    pad[...] = jnp.zeros_like(pad)
    blocks = acc.shape[0]
    if blocks > 18 * per:
        acc[18 * per:blocks] = jnp.zeros((blocks - 18 * per, 16, C), F32)
    pl.semaphore_wait(barrier, n_t * n_f - 1)

    start(0, x)
    await_arrivals(0, x)
    forward_taps(0, x, xf1)
    pre_one = apply(xf1, k1, 0)
    value, slope = gelu_parts(pre_one)
    backward_taps(0, x, xb)
    pre_grad = (apply(xb, k2, 1) * slope).astype(BF16)
    value = value.astype(BF16)
    for q in range(G):
        for j in range(J):
            m = (q * J + j) * H
            y[0, q, j] = value[m:m + H]
            y[1, q, j] = pre_grad[m:m + H]
    stage_rows(1, y)
    start(1, y)
    weight_terms(xf1, pre_grad, 0)
    await_arrivals(1, y)
    forward_taps(1, y, xf2)
    weight_terms(xf2, flat(x, 1), 9 * per)

    steps = []
    size = 1
    tile_bits, face_bits = [], []
    while size < n_t:
        tile_bits.append(size)
        size *= 2
    size = 1
    while size < n_f:
        face_bits.append(size)
        size *= 2
    order = [("tile", s) for s in tile_bits[:1]] + [("face", s) for s in face_bits] + [("tile", s) for s in tile_bits[1:]]

    def partner(axis, s):
        me = t if axis == "tile" else f
        bit = lax.rem(me // s, 2)
        other = me + (1 - 2 * bit) * s
        return bit, (where_to(other, f) if axis == "tile" else where_to(t, other))

    lo = 0
    length = blocks
    offset = 0
    for n, (axis, s) in enumerate(order):
        bit, dev = partner(axis, s)
        half = length // 2
        keep = lo + bit * half
        give = lo + (1 - bit) * half
        sbuf[pl.ds(give, half)] = acc[pl.ds(give, half)].astype(BF16)
        copy = remote(sbuf.at[pl.ds(give, half)], rbuf.at[offset:offset + half], w_s.at[n], w_r.at[n], dev)
        copy.start()
        if n == 0:
            out = apply(xf2, k2, 0).astype(BF16)
            for q in range(G):
                for j in range(J):
                    m = (q * J + j) * H
                    res_o[q, j] = out[m:m + H]
            backward_taps(1, y, xb)
            out = apply(xb, k1, 1).astype(BF16)
            for q in range(G):
                for j in range(J):
                    m = (q * J + j) * H
                    fg_o[q, j] = out[m:m + H]
        copy.wait()
        acc[pl.ds(keep, half)] += rbuf[offset:offset + half].astype(F32)
        steps.append((bit, dev, lo, keep, half))
        offset += half
        lo = keep
        length = half
    obuf[pl.ds(lo, length)] = acc[pl.ds(lo, length)].astype(BF16)
    for n, (bit, dev, before, keep, half) in reversed(list(enumerate(steps))):
        m = len(order) + n
        copy = remote(obuf.at[pl.ds(keep, half)], obuf.at[pl.ds(keep, half)], w_s.at[m], w_r.at[m], dev)
        copy.start()
        copy.wait()
    for n in range(9):
        w1_o[n] = obuf[n * per:(n + 1) * per].astype(F32).reshape(C, C)
        w2_o[n] = obuf[(9 + n) * per:(10 + n) * per].astype(F32).reshape(C, C)
    await_sends(0, x)
    await_sends(1, y)


def run(x, k1, k2, n_t, n_f):
    _, G, J, H, C = x.shape
    S = H // 3
    W = S + 16
    M = G * J * H
    ranks = n_t * n_f
    blocks = -(-(18 * (C // 16)) // ranks) * ranks
    scale = 1.0 / (S * 12.0 ** 0.5)
    bits = (n_t.bit_length() - 1) + (n_f.bit_length() - 1)
    dma = pltpu.SemaphoreType.DMA
    vmem = pl.BlockSpec(memory_space=pltpu.VMEM)
    return pl.pallas_call(
        functools.partial(body, n_t, n_f, scale),
        out_shape=(
            jax.ShapeDtypeStruct((G, J, H, C), BF16),
            jax.ShapeDtypeStruct((G, J, H, C), BF16),
            jax.ShapeDtypeStruct((9, C, C), F32),
            jax.ShapeDtypeStruct((9, C, C), F32),
        ),
        in_specs=[vmem] * 3,
        out_specs=[vmem] * 4,
        scratch_shapes=[
            pltpu.VMEM((2, G, J, H, C), BF16),
            pltpu.VMEM((2, 2, 2, G, J, C), F32),
            pltpu.VMEM((2, 2, G, H, C), BF16),
            pltpu.VMEM((2, 2, G, H, C), BF16),
            pltpu.VMEM((2, 2, G, W, C), BF16),
            pltpu.VMEM((2, 2, G, W, C), BF16),
            pltpu.VMEM((2, n_t, 2, G, J, C), F32),
            pltpu.VMEM((2, n_t, 2, G, J, C), F32),
            pltpu.VMEM((2, G, S + 16, C), F32),
            pltpu.VMEM((2, G, S + 16, C), F32),
            pltpu.VMEM((G, J + 2, H + 16, C), F32),
            pltpu.VMEM((9, M, C), F32),
            pltpu.VMEM((9, M, C), BF16),
            pltpu.VMEM((9, M, C), BF16),
            pltpu.VMEM((blocks, 16, C), F32),
            pltpu.VMEM((blocks, 16, C), BF16),
            pltpu.VMEM((blocks, 16, C), BF16),
            pltpu.VMEM((blocks, 16, C), BF16),
            dma((2, 6)), dma((2, 6)),
            dma((2, 2, n_t)), dma((2, 2)),
            dma((2, 2, n_t)), dma((2, 2)),
            dma((2, 2)), dma((2, 2, n_t)),
            dma((2, 2)), dma((2, 2, n_t)),
            dma((2 * bits,)), dma((2 * bits,)),
        ],
        compiler_params=pltpu.CompilerParams(
            collective_id=0, has_side_effects=True, vmem_limit_bytes=56 * 1024 * 1024),
    )(x, k1, k2)


def on_device(n_sub, n_t, n_f, fields, upstream, k1, k2):
    own = fields.shape[0]
    if n_sub > 1:
        fields = lax.all_gather(fields, "sub", axis=0, tiled=True)
        upstream = lax.all_gather(upstream, "sub", axis=0, tiled=True)
    x = jnp.stack([fields, upstream]).transpose(0, 2, 3, 4, 1)
    res, fgrad, w1, w2 = run(x, k1, k2, n_t, n_f)
    if n_sub > 1:
        at = lax.axis_index("sub") * own
        res = lax.dynamic_slice_in_dim(res, at, own, 3)
        fgrad = lax.dynamic_slice_in_dim(fgrad, at, own, 3)
        w1 = lax.dynamic_slice_in_dim(w1, at, own, 2)
        w2 = lax.dynamic_slice_in_dim(w2, at, own, 2)
    shape = (3, 3) + w1.shape[1:]
    return (res.transpose(3, 0, 1, 2), fgrad.transpose(3, 0, 1, 2), w1.reshape(shape), w2.reshape(shape))


def solution(mesh):
    placed = (P("sub", "face", "tile", "parts"), P("sub", "face", "tile", "parts"), P(), P())
    sizes = mesh.shape
    return jax.shard_map(
        functools.partial(on_device, sizes["sub"], sizes["tile"], sizes["face"]),
        mesh=mesh,
        in_specs=placed,
        out_specs=(
            P("sub", "face", "tile", "parts"),
            P("sub", "face", "tile", "parts"),
            P("parts", None, None, "sub"),
            P("parts", None, None, "sub"),
        ),
        check_vma=False,
    )
```

```python
import functools

import jax
import jax.numpy as jnp
from jax import lax
from jax.experimental import pallas as pl
from jax.experimental.pallas import tpu as pltpu
from jax.sharding import PartitionSpec as P

MESH = pl.DeviceIdType.MESH
F32 = jnp.float32
BF16 = jnp.bfloat16


def gelu_parts(v):
    root = 0.7978845608028654
    cube = 0.044715 * (v * v * v)
    th = jnp.tanh(root * (v + cube))
    value = v * (0.5 * (1.0 + th))
    slope = 0.5 * (1.0 + th) + 0.5 * v * (1.0 - th * th) * root * (1.0 + 0.134145 * (v * v))
    return value, slope


def product(a, b, da, db):
    return lax.dot_general(a, b, (((da,), (db,)), ((), ())), preferred_element_type=F32)


def body(n_t, n_f, scale, groups, x, k1, k2, res_o, fg_o, w1_o, w2_o,
         y, rows, lh, rh, ap, bm, aps, tr, dr, tl, dl, al, pad, xb, xf1, xf2,
         acc, sbuf, rlow, rfull, obuf,
         col_s, col_r, a_s, a_r, b_s, b_r, t_s, t_r, d_s, d_r, w_s, w_r):
    _, G, J, H, C = x.shape
    S = H // 3
    E = J + 2
    t = lax.axis_index("tile")
    f = lax.axis_index("face")
    fn = lax.rem(f + 1, n_f)
    fp = lax.rem(f + n_f - 1, n_f)
    first = t == 0
    last = t == n_t - 1
    inner_left = jnp.logical_not(first)
    inner_right = jnp.logical_not(last)

    def where_to(tile, face):
        return {"tile": tile, "face": face}

    def remote(src, dst, s, r, dev):
        return pltpu.make_async_remote_copy(
            src_ref=src, dst_ref=dst, send_sem=s, recv_sem=r, device_id=dev, device_id_type=MESH)

    def copies(p, src):
        c0, cl = src.at[:, 0], src.at[:, J - 1]
        right = lambda: remote(cl, lh.at[p], col_s.at[p, 0], col_r.at[p, 0], where_to(jnp.minimum(t + 1, n_t - 1), f))
        left = lambda: remote(c0, rh.at[p], col_s.at[p, 1], col_r.at[p, 1], where_to(jnp.maximum(t - 1, 0), f))
        seam = []
        if G > 1:
            seam.append((first, lambda: remote(src.at[1:G, 0], rh.at[p, 0:G - 1], col_s.at[p, 2], col_r.at[p, 2], where_to(n_t - 1, f))))
            seam.append((last, lambda: remote(src.at[0:G - 1, J - 1], lh.at[p, 1:G], col_s.at[p, 3], col_r.at[p, 3], where_to(0, f))))
        seam.append((first, lambda: remote(src.at[0:1, 0], rh.at[p, G - 1:G], col_s.at[p, 4], col_r.at[p, 4], where_to(n_t - 1, fp))))
        seam.append((last, lambda: remote(src.at[G - 1:G, J - 1], lh.at[p, 0:1], col_s.at[p, 5], col_r.at[p, 5], where_to(0, fn))))
        a_own = lambda d: remote(aps.at[p, d, 1:G], ap.at[p, 0:G - 1], a_s.at[p, 0, d], a_r.at[p, 0], where_to(d, f))
        a_oth = lambda d: remote(aps.at[p, d, 0:1], ap.at[p, G - 1:G], a_s.at[p, 1, d], a_r.at[p, 1], where_to(d, fp))
        b_own = lambda d: remote(aps.at[p, d, 0:G - 1], bm.at[p, 1:G], b_s.at[p, 0, d], b_r.at[p, 0], where_to(d, f))
        b_oth = lambda d: remote(aps.at[p, d, G - 1:G], bm.at[p, 0:1], b_s.at[p, 1, d], b_r.at[p, 1], where_to(d, fn))
        t_own = lambda d: remote(rows.at[p, 0, 0:G - 1], tr.at[p, d, 1:G], t_s.at[p, 0], t_r.at[p, 0, d], where_to(0, f))
        t_oth = lambda d: remote(rows.at[p, 0, G - 1:G], tr.at[p, d, 0:1], t_s.at[p, 1], t_r.at[p, 1, d], where_to(0, fn))
        d_own = lambda d: remote(rows.at[p, 1, 1:G], dr.at[p, d, 0:G - 1], d_s.at[p, 0], d_r.at[p, 0, d], where_to(n_t - 1, f))
        d_oth = lambda d: remote(rows.at[p, 1, 0:1], dr.at[p, d, G - 1:G], d_s.at[p, 1], d_r.at[p, 1, d], where_to(n_t - 1, fp))
        return right, left, seam, a_own, a_oth, b_own, b_oth, t_own, t_oth, d_own, d_oth

    def stage(p, src):
        for q in range(G):
            for j in range(J):
                rows[p, 0, q, j:j + 1, :] = src[q, j, 0:16].astype(F32)[0:1]
                rows[p, 1, q, j:j + 1, :] = src[q, j, H - 16:H].astype(F32)[15:16]

        @pl.when(first)
        def _():
            more = 16 * (p % 2)
            for q in range(G):
                al[p % 2, q, 16:16 + S + more, :] = src[q, 0, 0:S + more].astype(F32)
            for d in range(n_t):
                aps[p, d] = al[p % 2, :, 15 + d * J:15 + d * J + E, :]

        @pl.when(last)
        def _():
            more = 16 * (p % 2)
            for q in range(G):
                al[p % 2, q, 16 - more:16 + S, :] = src[q, J - 1, 2 * S - more:H].astype(F32)
            for d in range(n_t):
                aps[p, d] = al[p % 2, :, 15 + d * J:15 + d * J + E, :]

    def start(p, src):
        right, left, seam, a_own, a_oth, b_own, b_oth, t_own, t_oth, d_own, d_oth = copies(p, src)
        t_oth(t).start()
        d_oth(t).start()
        if G > 1:
            @pl.when(inner_left)
            def _():
                t_own(t).start()

            @pl.when(inner_right)
            def _():
                d_own(t).start()
        for cond, make in seam:
            @pl.when(cond)
            def _(make=make):
                make().start()

        @pl.when(first)
        def _():
            @pl.loop(0, n_t)
            def _(d):
                a_oth(n_t - 1 - d).start()
            if G > 1:
                @pl.loop(1, n_t)
                def _(d):
                    a_own(n_t - d).start()
                ap[p, 0:G - 1] = aps[p, 0, 1:G]
                tr[p, 0, 1:G] = rows[p, 0, 0:G - 1]

        @pl.when(last)
        def _():
            @pl.loop(0, n_t)
            def _(d):
                b_oth(d).start()
            if G > 1:
                @pl.loop(0, n_t - 1)
                def _(d):
                    b_own(d).start()
                bm[p, 1:G] = aps[p, n_t - 1, 0:G - 1]
                dr[p, n_t - 1, 0:G - 1] = rows[p, 1, 1:G]

        @pl.when(inner_right)
        def _():
            right().start()

        @pl.when(inner_left)
        def _():
            left().start()

    def await_arrivals(p, src):
        right, left, seam, a_own, a_oth, b_own, b_oth, t_own, t_oth, d_own, d_oth = copies(p, src)

        @pl.when(inner_left)
        def _():
            right().wait_recv()
            if G > 1:
                a_own(0).wait_recv()

        @pl.when(inner_right)
        def _():
            left().wait_recv()
            if G > 1:
                b_own(0).wait_recv()

        for cond, make in seam:
            @pl.when(last if cond is first else first)
            def _(make=make):
                make().wait_recv()

        a_oth(0).wait_recv()
        b_oth(0).wait_recv()

        @pl.when(first)
        def _():
            if G > 1:
                @pl.loop(1, n_t)
                def _(d):
                    t_own(d).wait_recv()

            @pl.loop(0, n_t)
            def _(d):
                t_oth(d).wait_recv()
            for d in range(n_t):
                tl[p % 2, :, 8 + d * J:8 + (d + 1) * J, :] = tr[p, d]

        @pl.when(last)
        def _():
            if G > 1:
                @pl.loop(0, n_t - 1)
                def _(d):
                    d_own(d).wait_recv()

            @pl.loop(0, n_t)
            def _(d):
                d_oth(d).wait_recv()
            for d in range(n_t):
                dl[p % 2, :, 8 + d * J:8 + (d + 1) * J, :] = dr[p, d]

    def await_sends(p, src):
        right, left, seam, a_own, a_oth, b_own, b_oth, t_own, t_oth, d_own, d_oth = copies(p, src)

        @pl.when(inner_right)
        def _():
            right().wait_send()
            if G > 1:
                d_own(t).wait_send()

        @pl.when(inner_left)
        def _():
            left().wait_send()
            if G > 1:
                t_own(t).wait_send()

        for cond, make in seam:
            @pl.when(cond)
            def _(make=make):
                make().wait_send()
        t_oth(t).wait_send()
        d_oth(t).wait_send()

        @pl.when(first)
        def _():
            if G > 1:
                @pl.loop(1, n_t)
                def _(d):
                    a_own(d).wait_send()

            @pl.loop(0, n_t)
            def _(d):
                a_oth(d).wait_send()

        @pl.when(last)
        def _():
            if G > 1:
                @pl.loop(0, n_t - 1)
                def _(d):
                    b_own(d).wait_send()

            @pl.loop(0, n_t)
            def _(d):
                b_oth(d).wait_send()

    def fill_columns(src):
        for q in range(G):
            for j in range(J):
                pad[q, 1 + j, 8:8 + H, :] = src[q, j].astype(F32)

    def forward_taps(p, src, out):
        fill_columns(src)
        for q in range(G):
            @pl.when(inner_left)
            def _():
                pad[q, 0, 8:8 + H, :] = lh[p, q].astype(F32)

            @pl.when(first)
            def _():
                pad[q, 0, 8:8 + S, :] = tl[0, q, 8:8 + S, :]
                pad[q, 0, 8 + S:8 + H, :] = lh[p, q, 0:2 * S].astype(F32)

            @pl.when(inner_right)
            def _():
                pad[q, J + 1, 8:8 + H, :] = rh[p, q].astype(F32)

            @pl.when(last)
            def _():
                pad[q, J + 1, 8:8 + 2 * S, :] = rh[p, q, S:H].astype(F32)
                pad[q, J + 1, 8 + 2 * S:8 + H, :] = dl[0, q, 8:8 + S, :]
            for j in range(E):
                pad[q, j, 7:8, :] = ap[p, q, j:j + 1]
                pad[q, j, 8 + H:9 + H, :] = bm[p, q, j:j + 1]
        for a in range(3):
            for b in range(3):
                for q in range(G):
                    for j in range(J):
                        m = (q * J + j) * H
                        out[3 * a + b, m:m + H, :] = pad[q, j + a, 7 + b:7 + b + H, :].astype(BF16)

    def backward_taps(p, src, out):
        fill_columns(src)
        for q in range(G):
            @pl.when(inner_left)
            def _():
                pad[q, 0, 8:8 + H, :] = lh[p, q].astype(F32)

            @pl.when(first)
            def _():
                pad[q, 0, :, :] = jnp.zeros((H + 16, C), F32)

            @pl.when(inner_right)
            def _():
                pad[q, J + 1, 8:8 + H, :] = rh[p, q].astype(F32)

            @pl.when(last)
            def _():
                pad[q, J + 1, :, :] = jnp.zeros((H + 16, C), F32)
            for j in range(E):
                pad[q, j, 7:8, :] = jnp.zeros((1, C), F32)
                pad[q, j, 8 + H:9 + H, :] = jnp.zeros((1, C), F32)
        for a in range(3):
            for b in range(3):
                for q in range(G):
                    for j in range(J):
                        m = (q * J + j) * H
                        out[3 * a + b, m:m + H, :] = pad[q, j - a + 2, 9 - b:9 - b + H, :]
        for q in range(G):
            top = ap[p, q]
            low = bm[p, q]
            for b in range(3):
                for j in range(J):
                    m = (q * J + j) * H
                    out[b, m:m + 1, :] += top[j + 2 - b:j + 3 - b]
                    out[6 + b, m + H - 1:m + H, :] += low[j + 2 - b:j + 3 - b]

        @pl.when(last)
        def _():
            for q in range(G):
                m = (q * J + J - 1) * H
                pad[q, J + 1, 8:8 + H, :] = rh[p, q].astype(F32)
                for e in range(3):
                    out[e, m:m + 2 * S, :] += pad[q, J + 1, 8 + S + 1 - e:8 + H + 1 - e, :]
                    out[3 * e + 2, m + 2 * S:m + H, :] += dl[1, q, 9 - e:9 - e + S, :]

        @pl.when(first)
        def _():
            for q in range(G):
                m = q * J * H
                pad[q, 0, 8:8 + H, :] = lh[p, q].astype(F32)
                for e in range(3):
                    out[3 * e, m:m + S, :] += tl[1, q, 9 - e:9 - e + S, :]
                    out[6 + e, m + S:m + H, :] += pad[q, 0, 9 - e:9 - e + 2 * S, :]

    def apply(taps, k, dim):
        total = product(taps[0].astype(BF16), k[0, 0], 1, dim)
        for n in range(1, 9):
            total = total + product(taps[n].astype(BF16), k[n // 3, n % 3], 1, dim)
        return total

    def flat(src):
        return jnp.concatenate([src[q, j] for q in range(G) for j in range(J)], axis=0)

    def unflat(value, dst):
        for q in range(G):
            for j in range(J):
                m = (q * J + j) * H
                dst[q, j] = value[m:m + H]

    per = C // 16
    blocks = acc.shape[1]

    def weight_terms(taps, cot, w):
        for n in range(9):
            term = product(taps[n], cot, 0, 0) * scale
            acc[w, n * per:(n + 1) * per] = term.reshape(per, 16, C)

    class Sum:
        def __init__(self, w):
            self.w, self.lo, self.length, self.done = w, 0, blocks, []
            self.used = [0, 0]
            self.sem = 0

        def members(self, bits):
            mine, place = [], 0
            for axis, s in bits:
                mine.append(lax.rem((t if axis == "tile" else f) // s, 2))
            found = []
            for k in range(1, 2 ** len(bits)):
                tile, face, digit = t, f, 0
                for pos, (axis, s) in enumerate(bits):
                    bit = mine[pos]
                    if (k >> pos) & 1:
                        if axis == "tile":
                            tile = tile + (1 - 2 * bit) * s
                        else:
                            face = face + (1 - 2 * bit) * s
                        bit = 1 - bit
                    digit = digit + bit * (1 << pos)
                found.append((digit, where_to(tile, face)))
            own = 0
            for pos, bit in enumerate(mine):
                own = own + bit * (1 << pos)
            return own, found

        def begin(self, n):
            bits, full = groups[n]
            own, found = self.members(bits)
            part = self.length // (len(found) + 1)
            w = self.w
            inbox = rfull if full else rlow
            self.flying = []
            for digit, dev in found:
                give = self.lo + digit * part
                at = self.used[full]
                self.used[full] += part
                if full:
                    out = acc.at[w, pl.ds(give, part)]
                else:
                    sbuf[w, pl.ds(give, part)] = acc[w, pl.ds(give, part)].astype(BF16)
                    out = sbuf.at[w, pl.ds(give, part)]
                copy = remote(out, inbox.at[w, at:at + part], w_s.at[w, self.sem], w_r.at[w, self.sem], dev)
                self.sem += 1
                copy.start()
                self.flying.append((copy, inbox, at))
            keep = self.lo + own * part
            self.done.append((keep, part, found))
            self.lo, self.length = keep, part

        def end(self):
            total = acc[self.w, pl.ds(self.lo, self.length)]
            for copy, inbox, at in self.flying:
                copy.wait()
                total = total + inbox[self.w, at:at + self.length].astype(F32)
            acc[self.w, pl.ds(self.lo, self.length)] = total

        def round(self):
            obuf[self.w, pl.ds(self.lo, self.length)] = acc[self.w, pl.ds(self.lo, self.length)].astype(BF16)

        def give(self, n):
            keep, part, found = self.done[n]
            self.flying = []
            for digit, dev in found:
                copy = remote(obuf.at[self.w, pl.ds(keep, part)], obuf.at[self.w, pl.ds(keep, part)],
                              w_s.at[self.w, self.sem], w_r.at[self.w, self.sem], dev)
                self.sem += 1
                copy.start()
                self.flying.append(copy)

        def given(self):
            for copy in self.flying:
                copy.wait()

    barrier = pltpu.get_barrier_semaphore()

    @pl.loop(0, n_f)
    def _(df):
        @pl.loop(0, n_t)
        def _(dt):
            @pl.when(jnp.logical_or(df != f, dt != t))
            def _():
                pl.semaphore_signal(barrier, inc=1, device_id=where_to(dt, df), device_id_type=MESH)
    fields, upstream, hidden, pre_grad = x.at[0], x.at[1], y.at[0], y.at[1]
    al[...] = jnp.zeros_like(al)
    tl[...] = jnp.zeros_like(tl)
    dl[...] = jnp.zeros_like(dl)
    stage(0, fields)
    stage(1, upstream)
    if blocks > 9 * per:
        for w in range(2):
            acc[w, 9 * per:blocks] = jnp.zeros((blocks - 9 * per, 16, C), F32)
    pl.semaphore_wait(barrier, n_t * n_f - 1)

    start(0, fields)
    start(1, upstream)
    await_arrivals(0, fields)
    forward_taps(0, fields, xf1)
    value, slope = gelu_parts(apply(xf1, k1, 0))
    unflat(value.astype(BF16), hidden)
    stage(2, hidden)
    start(2, hidden)
    await_arrivals(1, upstream)
    backward_taps(1, upstream, xb)
    cot = (apply(xb, k2, 1) * slope).astype(BF16)
    unflat(cot, pre_grad)
    stage(3, pre_grad)
    start(3, pre_grad)
    sums = [Sum(0), Sum(1)]
    weight_terms(xf1, cot, 0)
    sums[0].begin(0)
    await_arrivals(2, hidden)
    forward_taps(2, hidden, xf2)
    weight_terms(xf2, flat(upstream), 1)
    sums[1].begin(0)
    sums[0].end()
    if len(groups) > 1:
        sums[0].begin(1)
    unflat(apply(xf2, k2, 0).astype(BF16), res_o)
    sums[1].end()
    if len(groups) > 1:
        sums[1].begin(1)
    await_arrivals(3, pre_grad)
    backward_taps(3, pre_grad, xb)
    unflat(apply(xb, k1, 1).astype(BF16), fg_o)
    for n in range(1, len(groups)):
        for total in sums:
            total.end()
            if n + 1 < len(groups):
                total.begin(n + 1)
    for total in sums:
        total.round()
    for n in reversed(range(len(groups))):
        for total in sums:
            if n + 1 < len(groups):
                total.given()
            total.give(n)
    for total, out in zip(sums, (w1_o, w2_o)):
        total.given()
        for n in range(9):
            out[n] = obuf[total.w, n * per:(n + 1) * per].astype(F32).reshape(C, C)
    await_sends(0, fields)
    await_sends(1, upstream)
    await_sends(2, hidden)
    await_sends(3, pre_grad)


def plan(n_t, n_f):
    tile_bits = [1 << i for i in range(n_t.bit_length() - 1)]
    face_bits = [1 << i for i in range(n_f.bit_length() - 1)]
    groups = [([("tile", tile_bits[0])], 1)]
    middle = [("face", s) for s in face_bits] + [("tile", s) for s in tile_bits[1:2]]
    rest = [("tile", s) for s in tile_bits[2:]]
    while middle:
        groups.append((middle[:2], 0))
        middle = middle[2:]
    while rest:
        groups.append((rest[:2], 1))
        rest = rest[2:]
    return groups


def run(x, k1, k2, n_t, n_f):
    _, G, J, H, C = x.shape
    S = H // 3
    E = J + 2
    M = G * J * H
    ranks = n_t * n_f
    blocks = -(-(9 * (C // 16)) // ranks) * ranks
    scale = 1.0 / (S * 12.0 ** 0.5)
    groups = plan(n_t, n_f)
    length, room, flights = blocks, [1, 1], 0
    for bits, full in groups:
        others = 2 ** len(bits) - 1
        length //= others + 1
        room[full] += length * others
        flights += others
    dma = pltpu.SemaphoreType.DMA
    vmem = pl.BlockSpec(memory_space=pltpu.VMEM)
    return pl.pallas_call(
        functools.partial(body, n_t, n_f, scale, groups),
        out_shape=(
            jax.ShapeDtypeStruct((G, J, H, C), BF16),
            jax.ShapeDtypeStruct((G, J, H, C), BF16),
            jax.ShapeDtypeStruct((9, C, C), F32),
            jax.ShapeDtypeStruct((9, C, C), F32),
        ),
        in_specs=[vmem] * 3,
        out_specs=[vmem] * 4,
        scratch_shapes=[
            pltpu.VMEM((2, G, J, H, C), BF16),
            pltpu.VMEM((4, 2, G, J, C), F32),
            pltpu.VMEM((4, G, H, C), BF16),
            pltpu.VMEM((4, G, H, C), BF16),
            pltpu.VMEM((4, G, E, C), F32),
            pltpu.VMEM((4, G, E, C), F32),
            pltpu.VMEM((4, n_t, G, E, C), F32),
            pltpu.VMEM((4, n_t, G, J, C), F32),
            pltpu.VMEM((4, n_t, G, J, C), F32),
            pltpu.VMEM((2, G, S + 16, C), F32),
            pltpu.VMEM((2, G, S + 16, C), F32),
            pltpu.VMEM((2, G, S + 32, C), F32),
            pltpu.VMEM((G, J + 2, H + 16, C), F32),
            pltpu.VMEM((9, M, C), F32),
            pltpu.VMEM((9, M, C), BF16),
            pltpu.VMEM((9, M, C), BF16),
            pltpu.VMEM((2, blocks, 16, C), F32),
            pltpu.VMEM((2, blocks, 16, C), BF16),
            pltpu.VMEM((2, room[0], 16, C), BF16),
            pltpu.VMEM((2, room[1], 16, C), F32),
            pltpu.VMEM((2, blocks, 16, C), BF16),
            dma((4, 6)), dma((4, 6)),
            dma((4, 2, n_t)), dma((4, 2)),
            dma((4, 2, n_t)), dma((4, 2)),
            dma((4, 2)), dma((4, 2, n_t)),
            dma((4, 2)), dma((4, 2, n_t)),
            dma((2, 2 * flights)), dma((2, 2 * flights)),
        ],
        compiler_params=pltpu.CompilerParams(
            collective_id=0, has_side_effects=True, vmem_limit_bytes=56 * 1024 * 1024),
    )(x, k1, k2)


def on_device(n_sub, n_t, n_f, fields, upstream, k1, k2):
    own = fields.shape[0]
    if n_sub > 1:
        fields = lax.all_gather(fields, "sub", axis=0, tiled=True)
        upstream = lax.all_gather(upstream, "sub", axis=0, tiled=True)
    x = jnp.stack([fields, upstream]).transpose(0, 2, 3, 4, 1)
    res, fgrad, w1, w2 = run(x, k1, k2, n_t, n_f)
    if n_sub > 1:
        at = lax.axis_index("sub") * own
        res = lax.dynamic_slice_in_dim(res, at, own, 3)
        fgrad = lax.dynamic_slice_in_dim(fgrad, at, own, 3)
        w1 = lax.dynamic_slice_in_dim(w1, at, own, 2)
        w2 = lax.dynamic_slice_in_dim(w2, at, own, 2)
    shape = (3, 3) + w1.shape[1:]
    return (res.transpose(3, 0, 1, 2), fgrad.transpose(3, 0, 1, 2), w1.reshape(shape), w2.reshape(shape))


def solution(mesh):
    placed = (P("sub", "face", "tile", "parts"), P("sub", "face", "tile", "parts"), P(), P())
    sizes = mesh.shape
    return jax.shard_map(
        functools.partial(on_device, sizes["sub"], sizes["tile"], sizes["face"]),
        mesh=mesh,
        in_specs=placed,
        out_specs=(
            P("sub", "face", "tile", "parts"),
            P("sub", "face", "tile", "parts"),
            P("parts", None, None, "sub"),
            P("parts", None, None, "sub"),
        ),
        check_vma=False,
    )
```

```python
import functools

import jax
import jax.numpy as jnp
from jax import lax
from jax.experimental import pallas as pl
from jax.experimental.pallas import tpu as pltpu
from jax.sharding import PartitionSpec as P

MESH = pl.DeviceIdType.MESH
F32 = jnp.float32
BF16 = jnp.bfloat16


def gelu_parts(v):
    root = 0.7978845608028654
    cube = 0.044715 * (v * v * v)
    th = jnp.tanh(root * (v + cube))
    value = v * (0.5 * (1.0 + th))
    slope = 0.5 * (1.0 + th) + 0.5 * v * (1.0 - th * th) * root * (1.0 + 0.134145 * (v * v))
    return value, slope


def product(a, b, da, db):
    return lax.dot_general(a, b, (((da,), (db,)), ((), ())), preferred_element_type=F32)


def body(n_t, n_f, scale, groups, fields_h, upstream_h, k1_h, k2_h, res_o, fg_o, w1_o, w2_o,
         x, k1, k2, y, rows, lh, rh, ap, bm, aps, tr, dr, tl, dl, al, pad, xb, xf1, xf2,
         acc, sbuf, rlow, rfull, obuf,
         col_s, col_r, a_s, a_r, b_s, b_r, t_s, t_r, d_s, d_r, w_s, w_r, in_s):
    _, G, J, H, C = x.shape
    S = H // 3
    E = J + 2
    t = lax.axis_index("tile")
    f = lax.axis_index("face")
    fn = lax.rem(f + 1, n_f)
    fp = lax.rem(f + n_f - 1, n_f)
    first = t == 0
    last = t == n_t - 1
    inner_left = jnp.logical_not(first)
    inner_right = jnp.logical_not(last)

    def where_to(tile, face):
        return {"tile": tile, "face": face}

    def remote(src, dst, s, r, dev):
        return pltpu.make_async_remote_copy(
            src_ref=src, dst_ref=dst, send_sem=s, recv_sem=r, device_id=dev, device_id_type=MESH)

    def copies(p, src):
        c0, cl = src.at[:, 0], src.at[:, J - 1]
        right = lambda: remote(cl, lh.at[p], col_s.at[p, 0], col_r.at[p, 0], where_to(jnp.minimum(t + 1, n_t - 1), f))
        left = lambda: remote(c0, rh.at[p], col_s.at[p, 1], col_r.at[p, 1], where_to(jnp.maximum(t - 1, 0), f))
        seam = []
        if G > 1:
            seam.append((first, lambda: remote(src.at[1:G, 0], rh.at[p, 0:G - 1], col_s.at[p, 2], col_r.at[p, 2], where_to(n_t - 1, f))))
            seam.append((last, lambda: remote(src.at[0:G - 1, J - 1], lh.at[p, 1:G], col_s.at[p, 3], col_r.at[p, 3], where_to(0, f))))
        seam.append((first, lambda: remote(src.at[0:1, 0], rh.at[p, G - 1:G], col_s.at[p, 4], col_r.at[p, 4], where_to(n_t - 1, fp))))
        seam.append((last, lambda: remote(src.at[G - 1:G, J - 1], lh.at[p, 0:1], col_s.at[p, 5], col_r.at[p, 5], where_to(0, fn))))
        a_own = lambda d: remote(aps.at[p, d, 1:G], ap.at[p, 0:G - 1], a_s.at[p, 0, d], a_r.at[p, 0], where_to(d, f))
        a_oth = lambda d: remote(aps.at[p, d, 0:1], ap.at[p, G - 1:G], a_s.at[p, 1, d], a_r.at[p, 1], where_to(d, fp))
        b_own = lambda d: remote(aps.at[p, d, 0:G - 1], bm.at[p, 1:G], b_s.at[p, 0, d], b_r.at[p, 0], where_to(d, f))
        b_oth = lambda d: remote(aps.at[p, d, G - 1:G], bm.at[p, 0:1], b_s.at[p, 1, d], b_r.at[p, 1], where_to(d, fn))
        t_own = lambda d: remote(rows.at[p, 0, 0:G - 1], tr.at[p, d, 1:G], t_s.at[p, 0], t_r.at[p, 0, d], where_to(0, f))
        t_oth = lambda d: remote(rows.at[p, 0, G - 1:G], tr.at[p, d, 0:1], t_s.at[p, 1], t_r.at[p, 1, d], where_to(0, fn))
        d_own = lambda d: remote(rows.at[p, 1, 1:G], dr.at[p, d, 0:G - 1], d_s.at[p, 0], d_r.at[p, 0, d], where_to(n_t - 1, f))
        d_oth = lambda d: remote(rows.at[p, 1, 0:1], dr.at[p, d, G - 1:G], d_s.at[p, 1], d_r.at[p, 1, d], where_to(n_t - 1, fp))
        return right, left, seam, a_own, a_oth, b_own, b_oth, t_own, t_oth, d_own, d_oth

    def stage(p, src):
        for q in range(G):
            for j in range(J):
                rows[p, 0, q, j:j + 1, :] = src[q, j, 0:16].astype(F32)[0:1]
                rows[p, 1, q, j:j + 1, :] = src[q, j, H - 16:H].astype(F32)[15:16]

        @pl.when(first)
        def _():
            more = 16 * (p % 2)
            for q in range(G):
                al[p % 2, q, 16:16 + S + more, :] = src[q, 0, 0:S + more].astype(F32)
            for d in range(n_t):
                aps[p, d] = al[p % 2, :, 15 + d * J:15 + d * J + E, :]

        @pl.when(last)
        def _():
            more = 16 * (p % 2)
            for q in range(G):
                al[p % 2, q, 16 - more:16 + S, :] = src[q, J - 1, 2 * S - more:H].astype(F32)
            for d in range(n_t):
                aps[p, d] = al[p % 2, :, 15 + d * J:15 + d * J + E, :]

    def start(p, src):
        right, left, seam, a_own, a_oth, b_own, b_oth, t_own, t_oth, d_own, d_oth = copies(p, src)
        t_oth(t).start()
        d_oth(t).start()
        if G > 1:
            @pl.when(inner_left)
            def _():
                t_own(t).start()

            @pl.when(inner_right)
            def _():
                d_own(t).start()
        for cond, make in seam:
            @pl.when(cond)
            def _(make=make):
                make().start()

        @pl.when(first)
        def _():
            @pl.loop(0, n_t)
            def _(d):
                a_oth(n_t - 1 - d).start()
            if G > 1:
                @pl.loop(1, n_t)
                def _(d):
                    a_own(n_t - d).start()
                ap[p, 0:G - 1] = aps[p, 0, 1:G]
                tr[p, 0, 1:G] = rows[p, 0, 0:G - 1]

        @pl.when(last)
        def _():
            @pl.loop(0, n_t)
            def _(d):
                b_oth(d).start()
            if G > 1:
                @pl.loop(0, n_t - 1)
                def _(d):
                    b_own(d).start()
                bm[p, 1:G] = aps[p, n_t - 1, 0:G - 1]
                dr[p, n_t - 1, 0:G - 1] = rows[p, 1, 1:G]

        @pl.when(inner_right)
        def _():
            right().start()

        @pl.when(inner_left)
        def _():
            left().start()

    def await_arrivals(p, src):
        right, left, seam, a_own, a_oth, b_own, b_oth, t_own, t_oth, d_own, d_oth = copies(p, src)

        @pl.when(inner_left)
        def _():
            right().wait_recv()
            if G > 1:
                a_own(0).wait_recv()

        @pl.when(inner_right)
        def _():
            left().wait_recv()
            if G > 1:
                b_own(0).wait_recv()

        for cond, make in seam:
            @pl.when(last if cond is first else first)
            def _(make=make):
                make().wait_recv()

        a_oth(0).wait_recv()
        b_oth(0).wait_recv()

        @pl.when(first)
        def _():
            if G > 1:
                @pl.loop(1, n_t)
                def _(d):
                    t_own(d).wait_recv()

            @pl.loop(0, n_t)
            def _(d):
                t_oth(d).wait_recv()
            for d in range(n_t):
                tl[p % 2, :, 8 + d * J:8 + (d + 1) * J, :] = tr[p, d]

        @pl.when(last)
        def _():
            if G > 1:
                @pl.loop(0, n_t - 1)
                def _(d):
                    d_own(d).wait_recv()

            @pl.loop(0, n_t)
            def _(d):
                d_oth(d).wait_recv()
            for d in range(n_t):
                dl[p % 2, :, 8 + d * J:8 + (d + 1) * J, :] = dr[p, d]

    def await_sends(p, src):
        right, left, seam, a_own, a_oth, b_own, b_oth, t_own, t_oth, d_own, d_oth = copies(p, src)

        @pl.when(inner_right)
        def _():
            right().wait_send()
            if G > 1:
                d_own(t).wait_send()

        @pl.when(inner_left)
        def _():
            left().wait_send()
            if G > 1:
                t_own(t).wait_send()

        for cond, make in seam:
            @pl.when(cond)
            def _(make=make):
                make().wait_send()
        t_oth(t).wait_send()
        d_oth(t).wait_send()

        @pl.when(first)
        def _():
            if G > 1:
                @pl.loop(1, n_t)
                def _(d):
                    a_own(d).wait_send()

            @pl.loop(0, n_t)
            def _(d):
                a_oth(d).wait_send()

        @pl.when(last)
        def _():
            if G > 1:
                @pl.loop(0, n_t - 1)
                def _(d):
                    b_own(d).wait_send()

            @pl.loop(0, n_t)
            def _(d):
                b_oth(d).wait_send()

    def fill_columns(src):
        for q in range(G):
            for j in range(J):
                pad[q, 1 + j, 8:8 + H, :] = src[q, j].astype(F32)

    def forward_taps(p, src, out):
        fill_columns(src)
        for q in range(G):
            @pl.when(inner_left)
            def _():
                pad[q, 0, 8:8 + H, :] = lh[p, q].astype(F32)

            @pl.when(first)
            def _():
                pad[q, 0, 8:8 + S, :] = tl[0, q, 8:8 + S, :]
                pad[q, 0, 8 + S:8 + H, :] = lh[p, q, 0:2 * S].astype(F32)

            @pl.when(inner_right)
            def _():
                pad[q, J + 1, 8:8 + H, :] = rh[p, q].astype(F32)

            @pl.when(last)
            def _():
                pad[q, J + 1, 8:8 + 2 * S, :] = rh[p, q, S:H].astype(F32)
                pad[q, J + 1, 8 + 2 * S:8 + H, :] = dl[0, q, 8:8 + S, :]
            for j in range(E):
                pad[q, j, 7:8, :] = ap[p, q, j:j + 1]
                pad[q, j, 8 + H:9 + H, :] = bm[p, q, j:j + 1]
        for a in range(3):
            for b in range(3):
                for q in range(G):
                    for j in range(J):
                        m = (q * J + j) * H
                        out[3 * a + b, m:m + H, :] = pad[q, j + a, 7 + b:7 + b + H, :].astype(BF16)

    def backward_taps(p, src, out):
        fill_columns(src)
        for q in range(G):
            @pl.when(inner_left)
            def _():
                pad[q, 0, 8:8 + H, :] = lh[p, q].astype(F32)

            @pl.when(first)
            def _():
                pad[q, 0, :, :] = jnp.zeros((H + 16, C), F32)

            @pl.when(inner_right)
            def _():
                pad[q, J + 1, 8:8 + H, :] = rh[p, q].astype(F32)

            @pl.when(last)
            def _():
                pad[q, J + 1, :, :] = jnp.zeros((H + 16, C), F32)
            for j in range(E):
                pad[q, j, 7:8, :] = jnp.zeros((1, C), F32)
                pad[q, j, 8 + H:9 + H, :] = jnp.zeros((1, C), F32)
        for a in range(3):
            for b in range(3):
                for q in range(G):
                    for j in range(J):
                        m = (q * J + j) * H
                        out[3 * a + b, m:m + H, :] = pad[q, j - a + 2, 9 - b:9 - b + H, :]
        for q in range(G):
            top = ap[p, q]
            low = bm[p, q]
            for b in range(3):
                for j in range(J):
                    m = (q * J + j) * H
                    out[b, m:m + 1, :] += top[j + 2 - b:j + 3 - b]
                    out[6 + b, m + H - 1:m + H, :] += low[j + 2 - b:j + 3 - b]

        @pl.when(last)
        def _():
            for q in range(G):
                m = (q * J + J - 1) * H
                pad[q, J + 1, 8:8 + H, :] = rh[p, q].astype(F32)
                for e in range(3):
                    out[e, m:m + 2 * S, :] += pad[q, J + 1, 8 + S + 1 - e:8 + H + 1 - e, :]
                    out[3 * e + 2, m + 2 * S:m + H, :] += dl[1, q, 9 - e:9 - e + S, :]

        @pl.when(first)
        def _():
            for q in range(G):
                m = q * J * H
                pad[q, 0, 8:8 + H, :] = lh[p, q].astype(F32)
                for e in range(3):
                    out[3 * e, m:m + S, :] += tl[1, q, 9 - e:9 - e + S, :]
                    out[6 + e, m + S:m + H, :] += pad[q, 0, 9 - e:9 - e + 2 * S, :]

    def apply(taps, k, dim):
        total = product(taps[0].astype(BF16), k[0, 0], 1, dim)
        for n in range(1, 9):
            total = total + product(taps[n].astype(BF16), k[n // 3, n % 3], 1, dim)
        return total

    def flat(src):
        return jnp.concatenate([src[q, j] for q in range(G) for j in range(J)], axis=0)

    def unflat(value, dst):
        for q in range(G):
            for j in range(J):
                m = (q * J + j) * H
                dst[q, j] = value[m:m + H]

    per = C // 16
    blocks = acc.shape[1]

    def weight_terms(taps, cot, w):
        for n in range(9):
            term = product(taps[n], cot, 0, 0) * scale
            acc[w, n * per:(n + 1) * per] = term.reshape(per, 16, C)

    class Sum:
        def __init__(self, w):
            self.w, self.lo, self.length, self.done = w, 0, blocks, []
            self.used = [0, 0]
            self.sem = 0

        def members(self, bits):
            mine, place = [], 0
            for axis, s in bits:
                mine.append(lax.rem((t if axis == "tile" else f) // s, 2))
            found = []
            for k in range(1, 2 ** len(bits)):
                tile, face, digit = t, f, 0
                for pos, (axis, s) in enumerate(bits):
                    bit = mine[pos]
                    if (k >> pos) & 1:
                        if axis == "tile":
                            tile = tile + (1 - 2 * bit) * s
                        else:
                            face = face + (1 - 2 * bit) * s
                        bit = 1 - bit
                    digit = digit + bit * (1 << pos)
                found.append((digit, where_to(tile, face)))
            own = 0
            for pos, bit in enumerate(mine):
                own = own + bit * (1 << pos)
            return own, found

        def begin(self, n):
            bits, full = groups[n]
            own, found = self.members(bits)
            part = self.length // (len(found) + 1)
            w = self.w
            inbox = rfull if full else rlow
            self.flying = []
            for digit, dev in found:
                give = self.lo + digit * part
                at = self.used[full]
                self.used[full] += part
                if full:
                    out = acc.at[w, pl.ds(give, part)]
                else:
                    sbuf[w, pl.ds(give, part)] = acc[w, pl.ds(give, part)].astype(BF16)
                    out = sbuf.at[w, pl.ds(give, part)]
                copy = remote(out, inbox.at[w, at:at + part], w_s.at[w, self.sem], w_r.at[w, self.sem], dev)
                self.sem += 1
                copy.start()
                self.flying.append((copy, inbox, at))
            keep = self.lo + own * part
            self.done.append((keep, part, found))
            self.lo, self.length = keep, part

        def end(self):
            total = acc[self.w, pl.ds(self.lo, self.length)]
            for copy, inbox, at in self.flying:
                copy.wait()
                total = total + inbox[self.w, at:at + self.length].astype(F32)
            acc[self.w, pl.ds(self.lo, self.length)] = total

        def round(self):
            obuf[self.w, pl.ds(self.lo, self.length)] = acc[self.w, pl.ds(self.lo, self.length)].astype(BF16)

        def give(self, n):
            keep, part, found = self.done[n]
            self.flying = []
            for digit, dev in found:
                copy = remote(obuf.at[self.w, pl.ds(keep, part)], obuf.at[self.w, pl.ds(keep, part)],
                              w_s.at[self.w, self.sem], w_r.at[self.w, self.sem], dev)
                self.sem += 1
                copy.start()
                self.flying.append(copy)

        def given(self):
            for copy in self.flying:
                copy.wait()

    barrier = pltpu.get_barrier_semaphore()

    @pl.loop(0, n_f)
    def _(df):
        @pl.loop(0, n_t)
        def _(dt):
            @pl.when(jnp.logical_or(df != f, dt != t))
            def _():
                pl.semaphore_signal(barrier, inc=1, device_id=where_to(dt, df), device_id_type=MESH)
    loads = [pltpu.make_async_copy(src, dst, in_s.at[n]) for n, (src, dst) in enumerate(
        ((fields_h, x.at[0]), (upstream_h, x.at[1]), (k1_h, k1), (k2_h, k2)))]
    for load in loads:
        load.start()
    fields, upstream, hidden, pre_grad = x.at[0], x.at[1], y.at[0], y.at[1]
    al[...] = jnp.zeros_like(al)
    tl[...] = jnp.zeros_like(tl)
    dl[...] = jnp.zeros_like(dl)
    loads[0].wait()
    loads[1].wait()
    stage(0, fields)
    stage(1, upstream)
    if blocks > 9 * per:
        for w in range(2):
            acc[w, 9 * per:blocks] = jnp.zeros((blocks - 9 * per, 16, C), F32)
    pl.semaphore_wait(barrier, n_t * n_f - 1)

    start(0, fields)
    start(1, upstream)
    loads[2].wait()
    loads[3].wait()
    await_arrivals(0, fields)
    forward_taps(0, fields, xf1)
    value, slope = gelu_parts(apply(xf1, k1, 0))
    unflat(value.astype(BF16), hidden)
    stage(2, hidden)
    start(2, hidden)
    await_arrivals(1, upstream)
    backward_taps(1, upstream, xb)
    cot = (apply(xb, k2, 1) * slope).astype(BF16)
    unflat(cot, pre_grad)
    stage(3, pre_grad)
    start(3, pre_grad)
    sums = [Sum(0), Sum(1)]
    weight_terms(xf1, cot, 0)
    sums[0].begin(0)
    await_arrivals(2, hidden)
    forward_taps(2, hidden, xf2)
    weight_terms(xf2, flat(upstream), 1)
    sums[1].begin(0)
    sums[0].end()
    if len(groups) > 1:
        sums[0].begin(1)
    unflat(apply(xf2, k2, 0).astype(BF16), res_o)
    sums[1].end()
    if len(groups) > 1:
        sums[1].begin(1)
    await_arrivals(3, pre_grad)
    backward_taps(3, pre_grad, xb)
    unflat(apply(xb, k1, 1).astype(BF16), fg_o)
    for n in range(1, len(groups)):
        for total in sums:
            total.end()
            if n + 1 < len(groups):
                total.begin(n + 1)
    for total in sums:
        total.round()
    for n in reversed(range(len(groups))):
        for total in sums:
            if n + 1 < len(groups):
                total.given()
            total.give(n)
    for total, out in zip(sums, (w1_o, w2_o)):
        total.given()
        for n in range(9):
            out[n] = obuf[total.w, n * per:(n + 1) * per].reshape(C, C)
    await_sends(0, fields)
    await_sends(1, upstream)
    await_sends(2, hidden)
    await_sends(3, pre_grad)


def plan(n_t, n_f):
    tile_bits = [1 << i for i in range(n_t.bit_length() - 1)]
    face_bits = [1 << i for i in range(n_f.bit_length() - 1)]
    groups = [([("tile", tile_bits[0])], 1)]
    middle = [("face", s) for s in face_bits] + [("tile", s) for s in tile_bits[1:2]]
    rest = [("tile", s) for s in tile_bits[2:]]
    while middle:
        groups.append((middle[:2], 0))
        middle = middle[2:]
    while rest:
        groups.append((rest[:2], 0))
        rest = rest[2:]
    return groups


def run(fields, upstream, k1, k2, n_t, n_f):
    G, J, H, C = fields.shape
    S = H // 3
    E = J + 2
    M = G * J * H
    ranks = n_t * n_f
    blocks = -(-(9 * (C // 16)) // ranks) * ranks
    scale = 1.0 / (S * 12.0 ** 0.5)
    groups = plan(n_t, n_f)
    length, room, flights = blocks, [1, 1], 0
    for bits, full in groups:
        others = 2 ** len(bits) - 1
        length //= others + 1
        room[full] += length * others
        flights += others
    dma = pltpu.SemaphoreType.DMA
    vmem = pl.BlockSpec(memory_space=pltpu.VMEM)
    return pl.pallas_call(
        functools.partial(body, n_t, n_f, scale, groups),
        out_shape=(
            jax.ShapeDtypeStruct((G, J, H, C), BF16),
            jax.ShapeDtypeStruct((G, J, H, C), BF16),
            jax.ShapeDtypeStruct((9, C, C), BF16),
            jax.ShapeDtypeStruct((9, C, C), BF16),
        ),
        in_specs=[pl.BlockSpec(memory_space=pl.ANY)] * 2 + [pl.BlockSpec(memory_space=pltpu.HBM)] * 2,
        out_specs=[vmem] * 4,
        scratch_shapes=[
            pltpu.VMEM((2, G, J, H, C), BF16),
            pltpu.VMEM(k1.shape, BF16),
            pltpu.VMEM(k2.shape, BF16),
            pltpu.VMEM((2, G, J, H, C), BF16),
            pltpu.VMEM((4, 2, G, J, C), F32),
            pltpu.VMEM((4, G, H, C), BF16),
            pltpu.VMEM((4, G, H, C), BF16),
            pltpu.VMEM((4, G, E, C), F32),
            pltpu.VMEM((4, G, E, C), F32),
            pltpu.VMEM((4, n_t, G, E, C), F32),
            pltpu.VMEM((4, n_t, G, J, C), F32),
            pltpu.VMEM((4, n_t, G, J, C), F32),
            pltpu.VMEM((2, G, S + 16, C), F32),
            pltpu.VMEM((2, G, S + 16, C), F32),
            pltpu.VMEM((2, G, S + 32, C), F32),
            pltpu.VMEM((G, J + 2, H + 16, C), F32),
            pltpu.VMEM((9, M, C), F32),
            pltpu.VMEM((9, M, C), BF16),
            pltpu.VMEM((9, M, C), BF16),
            pltpu.VMEM((2, blocks, 16, C), F32),
            pltpu.VMEM((2, blocks, 16, C), BF16),
            pltpu.VMEM((2, room[0], 16, C), BF16),
            pltpu.VMEM((2, room[1], 16, C), F32),
            pltpu.VMEM((2, blocks, 16, C), BF16),
            dma((4, 6)), dma((4, 6)),
            dma((4, 2, n_t)), dma((4, 2)),
            dma((4, 2, n_t)), dma((4, 2)),
            dma((4, 2)), dma((4, 2, n_t)),
            dma((4, 2)), dma((4, 2, n_t)),
            dma((2, 2 * flights)), dma((2, 2 * flights)), dma((4,)),
        ],
        compiler_params=pltpu.CompilerParams(
            collective_id=0, has_side_effects=True, vmem_limit_bytes=24 * 1024 * 1024),
    )(fields, upstream, k1, k2)


def on_device(n_sub, n_t, n_f, fields, upstream, k1, k2):
    own = fields.shape[0]
    if n_sub > 1:
        fields = lax.all_gather(fields, "sub", axis=0, tiled=True)
        upstream = lax.all_gather(upstream, "sub", axis=0, tiled=True)
    res, fgrad, w1, w2 = run(
        fields.transpose(1, 2, 3, 0), upstream.transpose(1, 2, 3, 0), k1, k2, n_t, n_f)
    if n_sub > 1:
        at = lax.axis_index("sub") * own
        res = lax.dynamic_slice_in_dim(res, at, own, 3)
        fgrad = lax.dynamic_slice_in_dim(fgrad, at, own, 3)
        w1 = lax.dynamic_slice_in_dim(w1, at, own, 2)
        w2 = lax.dynamic_slice_in_dim(w2, at, own, 2)
    shape = (3, 3) + w1.shape[1:]
    return (res.transpose(3, 0, 1, 2), fgrad.transpose(3, 0, 1, 2), w1.astype(F32).reshape(shape), w2.astype(F32).reshape(shape))


def solution(mesh):
    placed = (P("sub", "face", "tile", "parts"), P("sub", "face", "tile", "parts"), P(), P())
    sizes = mesh.shape
    return jax.shard_map(
        functools.partial(on_device, sizes["sub"], sizes["tile"], sizes["face"]),
        mesh=mesh,
        in_specs=placed,
        out_specs=(
            P("sub", "face", "tile", "parts"),
            P("sub", "face", "tile", "parts"),
            P("parts", None, None, "sub"),
            P("parts", None, None, "sub"),
        ),
        check_vma=False,
    )
```

```python
import functools

import jax
import jax.numpy as jnp
from jax import lax
from jax.experimental import pallas as pl
from jax.experimental.pallas import tpu as pltpu
from jax.sharding import PartitionSpec as P

MESH = pl.DeviceIdType.MESH
F32 = jnp.float32
BF16 = jnp.bfloat16


def gelu_parts(v):
    root = 0.7978845608028654
    cube = 0.044715 * (v * v * v)
    th = jnp.tanh(root * (v + cube))
    value = v * (0.5 * (1.0 + th))
    slope = 0.5 * (1.0 + th) + 0.5 * v * (1.0 - th * th) * root * (1.0 + 0.134145 * (v * v))
    return value, slope


def product(a, b, da, db):
    return lax.dot_general(a, b, (((da,), (db,)), ((), ())), preferred_element_type=F32)


def body(n_t, n_f, scale, groups, fields_h, upstream_h, k1_h, k2_h, res_o, fg_o, w1_o, w2_o,
         x, k1, k2, y, rows, lh, rh, ap, bm, aps, tr, dr, tl, dl, al, pad, xb, xf1, xf2,
         acc, sbuf, rlow, rfull, obuf,
         col_s, col_r, a_s, a_r, b_s, b_r, t_s, t_r, d_s, d_r, w_s, w_r, in_s):
    _, G, J, H, C = x.shape
    S = H // 3
    E = J + 2
    t = lax.axis_index("tile")
    f = lax.axis_index("face")
    fn = lax.rem(f + 1, n_f)
    fp = lax.rem(f + n_f - 1, n_f)
    first = t == 0
    last = t == n_t - 1
    inner_left = jnp.logical_not(first)
    inner_right = jnp.logical_not(last)

    def where_to(tile, face):
        return {"tile": tile, "face": face}

    def remote(src, dst, s, r, dev):
        return pltpu.make_async_remote_copy(
            src_ref=src, dst_ref=dst, send_sem=s, recv_sem=r, device_id=dev, device_id_type=MESH)

    def copies(p, src):
        c0, cl = src.at[:, 0], src.at[:, J - 1]
        right = lambda: remote(cl, lh.at[p], col_s.at[p, 0], col_r.at[p, 0], where_to(jnp.minimum(t + 1, n_t - 1), f))
        left = lambda: remote(c0, rh.at[p], col_s.at[p, 1], col_r.at[p, 1], where_to(jnp.maximum(t - 1, 0), f))
        seam = []
        if G > 1:
            seam.append((first, lambda: remote(src.at[1:G, 0], rh.at[p, 0:G - 1], col_s.at[p, 2], col_r.at[p, 2], where_to(n_t - 1, f))))
            seam.append((last, lambda: remote(src.at[0:G - 1, J - 1], lh.at[p, 1:G], col_s.at[p, 3], col_r.at[p, 3], where_to(0, f))))
        seam.append((first, lambda: remote(src.at[0:1, 0], rh.at[p, G - 1:G], col_s.at[p, 4], col_r.at[p, 4], where_to(n_t - 1, fp))))
        seam.append((last, lambda: remote(src.at[G - 1:G, J - 1], lh.at[p, 0:1], col_s.at[p, 5], col_r.at[p, 5], where_to(0, fn))))
        a_own = lambda d: remote(aps.at[p, d, 1:G], ap.at[p, 0:G - 1], a_s.at[p, 0, d], a_r.at[p, 0], where_to(d, f))
        a_oth = lambda d: remote(aps.at[p, d, 0:1], ap.at[p, G - 1:G], a_s.at[p, 1, d], a_r.at[p, 1], where_to(d, fp))
        b_own = lambda d: remote(aps.at[p, d, 0:G - 1], bm.at[p, 1:G], b_s.at[p, 0, d], b_r.at[p, 0], where_to(d, f))
        b_oth = lambda d: remote(aps.at[p, d, G - 1:G], bm.at[p, 0:1], b_s.at[p, 1, d], b_r.at[p, 1], where_to(d, fn))
        t_own = lambda d: remote(rows.at[p, 0, 0:G - 1], tr.at[p, d, 1:G], t_s.at[p, 0], t_r.at[p, 0, d], where_to(0, f))
        t_oth = lambda d: remote(rows.at[p, 0, G - 1:G], tr.at[p, d, 0:1], t_s.at[p, 1], t_r.at[p, 1, d], where_to(0, fn))
        d_own = lambda d: remote(rows.at[p, 1, 1:G], dr.at[p, d, 0:G - 1], d_s.at[p, 0], d_r.at[p, 0, d], where_to(n_t - 1, f))
        d_oth = lambda d: remote(rows.at[p, 1, 0:1], dr.at[p, d, G - 1:G], d_s.at[p, 1], d_r.at[p, 1, d], where_to(n_t - 1, fp))
        return right, left, seam, a_own, a_oth, b_own, b_oth, t_own, t_oth, d_own, d_oth

    def stage(p, src):
        for q in range(G):
            for j in range(J):
                rows[p, 0, q, j:j + 1, :] = src[q, j, 0:16].astype(F32)[0:1]
                rows[p, 1, q, j:j + 1, :] = src[q, j, H - 16:H].astype(F32)[15:16]

        @pl.when(first)
        def _():
            more = 16 * (p % 2)
            for q in range(G):
                al[p % 2, q, 16:16 + S + more, :] = src[q, 0, 0:S + more].astype(F32)
            for d in range(n_t):
                aps[p, d] = al[p % 2, :, 15 + d * J:15 + d * J + E, :]

        @pl.when(last)
        def _():
            more = 16 * (p % 2)
            for q in range(G):
                al[p % 2, q, 16 - more:16 + S, :] = src[q, J - 1, 2 * S - more:H].astype(F32)
            for d in range(n_t):
                aps[p, d] = al[p % 2, :, 15 + d * J:15 + d * J + E, :]

    def start(p, src):
        right, left, seam, a_own, a_oth, b_own, b_oth, t_own, t_oth, d_own, d_oth = copies(p, src)
        t_oth(t).start()
        d_oth(t).start()
        if G > 1:
            @pl.when(inner_left)
            def _():
                t_own(t).start()

            @pl.when(inner_right)
            def _():
                d_own(t).start()
        for cond, make in seam:
            @pl.when(cond)
            def _(make=make):
                make().start()

        @pl.when(first)
        def _():
            @pl.loop(0, n_t)
            def _(d):
                a_oth(n_t - 1 - d).start()
            if G > 1:
                @pl.loop(1, n_t)
                def _(d):
                    a_own(n_t - d).start()
                ap[p, 0:G - 1] = aps[p, 0, 1:G]
                tr[p, 0, 1:G] = rows[p, 0, 0:G - 1]

        @pl.when(last)
        def _():
            @pl.loop(0, n_t)
            def _(d):
                b_oth(d).start()
            if G > 1:
                @pl.loop(0, n_t - 1)
                def _(d):
                    b_own(d).start()
                bm[p, 1:G] = aps[p, n_t - 1, 0:G - 1]
                dr[p, n_t - 1, 0:G - 1] = rows[p, 1, 1:G]

        @pl.when(inner_right)
        def _():
            right().start()

        @pl.when(inner_left)
        def _():
            left().start()

    def await_arrivals(p, src):
        right, left, seam, a_own, a_oth, b_own, b_oth, t_own, t_oth, d_own, d_oth = copies(p, src)

        @pl.when(inner_left)
        def _():
            right().wait_recv()
            if G > 1:
                a_own(0).wait_recv()

        @pl.when(inner_right)
        def _():
            left().wait_recv()
            if G > 1:
                b_own(0).wait_recv()

        for cond, make in seam:
            @pl.when(last if cond is first else first)
            def _(make=make):
                make().wait_recv()

        a_oth(0).wait_recv()
        b_oth(0).wait_recv()

        @pl.when(first)
        def _():
            if G > 1:
                @pl.loop(1, n_t)
                def _(d):
                    t_own(d).wait_recv()

            @pl.loop(0, n_t)
            def _(d):
                t_oth(d).wait_recv()
            for d in range(n_t):
                tl[p % 2, :, 8 + d * J:8 + (d + 1) * J, :] = tr[p, d]

        @pl.when(last)
        def _():
            if G > 1:
                @pl.loop(0, n_t - 1)
                def _(d):
                    d_own(d).wait_recv()

            @pl.loop(0, n_t)
            def _(d):
                d_oth(d).wait_recv()
            for d in range(n_t):
                dl[p % 2, :, 8 + d * J:8 + (d + 1) * J, :] = dr[p, d]

    def await_sends(p, src):
        right, left, seam, a_own, a_oth, b_own, b_oth, t_own, t_oth, d_own, d_oth = copies(p, src)

        @pl.when(inner_right)
        def _():
            right().wait_send()
            if G > 1:
                d_own(t).wait_send()

        @pl.when(inner_left)
        def _():
            left().wait_send()
            if G > 1:
                t_own(t).wait_send()

        for cond, make in seam:
            @pl.when(cond)
            def _(make=make):
                make().wait_send()
        t_oth(t).wait_send()
        d_oth(t).wait_send()

        @pl.when(first)
        def _():
            if G > 1:
                @pl.loop(1, n_t)
                def _(d):
                    a_own(d).wait_send()

            @pl.loop(0, n_t)
            def _(d):
                a_oth(d).wait_send()

        @pl.when(last)
        def _():
            if G > 1:
                @pl.loop(0, n_t - 1)
                def _(d):
                    b_own(d).wait_send()

            @pl.loop(0, n_t)
            def _(d):
                b_oth(d).wait_send()

    def fill_columns(src):
        for q in range(G):
            for j in range(J):
                pad[q, 1 + j, 8:8 + H, :] = src[q, j].astype(F32)

    def forward_taps(p, src, out):
        fill_columns(src)
        for q in range(G):
            @pl.when(inner_left)
            def _():
                pad[q, 0, 8:8 + H, :] = lh[p, q].astype(F32)

            @pl.when(first)
            def _():
                pad[q, 0, 8:8 + S, :] = tl[0, q, 8:8 + S, :]
                pad[q, 0, 8 + S:8 + H, :] = lh[p, q, 0:2 * S].astype(F32)

            @pl.when(inner_right)
            def _():
                pad[q, J + 1, 8:8 + H, :] = rh[p, q].astype(F32)

            @pl.when(last)
            def _():
                pad[q, J + 1, 8:8 + 2 * S, :] = rh[p, q, S:H].astype(F32)
                pad[q, J + 1, 8 + 2 * S:8 + H, :] = dl[0, q, 8:8 + S, :]
            for j in range(E):
                pad[q, j, 7:8, :] = ap[p, q, j:j + 1]
                pad[q, j, 8 + H:9 + H, :] = bm[p, q, j:j + 1]
        for a in range(3):
            for b in range(3):
                for q in range(G):
                    for j in range(J):
                        m = (q * J + j) * H
                        out[3 * a + b, m:m + H, :] = pad[q, j + a, 7 + b:7 + b + H, :].astype(BF16)

    def backward_taps(p, src, out):
        fill_columns(src)
        for q in range(G):
            @pl.when(inner_left)
            def _():
                pad[q, 0, 8:8 + H, :] = lh[p, q].astype(F32)

            @pl.when(first)
            def _():
                pad[q, 0, :, :] = jnp.zeros((H + 16, C), F32)

            @pl.when(inner_right)
            def _():
                pad[q, J + 1, 8:8 + H, :] = rh[p, q].astype(F32)

            @pl.when(last)
            def _():
                pad[q, J + 1, :, :] = jnp.zeros((H + 16, C), F32)
            for j in range(E):
                pad[q, j, 7:8, :] = jnp.zeros((1, C), F32)
                pad[q, j, 8 + H:9 + H, :] = jnp.zeros((1, C), F32)
        for a in range(3):
            for b in range(3):
                for q in range(G):
                    for j in range(J):
                        m = (q * J + j) * H
                        out[3 * a + b, m:m + H, :] = pad[q, j - a + 2, 9 - b:9 - b + H, :]
        for q in range(G):
            top = ap[p, q]
            low = bm[p, q]
            for b in range(3):
                for j in range(J):
                    m = (q * J + j) * H
                    out[b, m:m + 1, :] += top[j + 2 - b:j + 3 - b]
                    out[6 + b, m + H - 1:m + H, :] += low[j + 2 - b:j + 3 - b]

        @pl.when(last)
        def _():
            for q in range(G):
                m = (q * J + J - 1) * H
                pad[q, J + 1, 8:8 + H, :] = rh[p, q].astype(F32)
                for e in range(3):
                    out[e, m:m + 2 * S, :] += pad[q, J + 1, 8 + S + 1 - e:8 + H + 1 - e, :]
                    out[3 * e + 2, m + 2 * S:m + H, :] += dl[1, q, 9 - e:9 - e + S, :]

        @pl.when(first)
        def _():
            for q in range(G):
                m = q * J * H
                pad[q, 0, 8:8 + H, :] = lh[p, q].astype(F32)
                for e in range(3):
                    out[3 * e, m:m + S, :] += tl[1, q, 9 - e:9 - e + S, :]
                    out[6 + e, m + S:m + H, :] += pad[q, 0, 9 - e:9 - e + 2 * S, :]

    def apply(taps, k, dim):
        total = product(taps[0].astype(BF16), k[0, 0], 1, dim)
        for n in range(1, 9):
            total = total + product(taps[n].astype(BF16), k[n // 3, n % 3], 1, dim)
        return total

    def flat(src):
        return jnp.concatenate([src[q, j] for q in range(G) for j in range(J)], axis=0)

    def unflat(value, dst):
        for q in range(G):
            for j in range(J):
                m = (q * J + j) * H
                dst[q, j] = value[m:m + H]

    per = C // 16
    blocks = acc.shape[1]

    def weight_terms(taps, cot, w):
        for n in range(9):
            term = product(taps[n], cot, 0, 0) * scale
            acc[w, n * per:(n + 1) * per] = term.reshape(per, 16, C)

    class Sum:
        def __init__(self, w, out):
            self.out, self.at, self.over = out, 0, False
            self.w, self.lo, self.length, self.done = w, 0, blocks, []
            self.used = [0, 0]
            self.sem = 0

        def members(self, bits):
            mine, place = [], 0
            for axis, s in bits:
                mine.append(lax.rem((t if axis == "tile" else f) // s, 2))
            found = []
            for k in range(1, 2 ** len(bits)):
                tile, face, digit = t, f, 0
                for pos, (axis, s) in enumerate(bits):
                    bit = mine[pos]
                    if (k >> pos) & 1:
                        if axis == "tile":
                            tile = tile + (1 - 2 * bit) * s
                        else:
                            face = face + (1 - 2 * bit) * s
                        bit = 1 - bit
                    digit = digit + bit * (1 << pos)
                found.append((digit, where_to(tile, face)))
            own = 0
            for pos, bit in enumerate(mine):
                own = own + bit * (1 << pos)
            return own, found

        def begin(self, n):
            bits, full = groups[n]
            own, found = self.members(bits)
            part = self.length // (len(found) + 1)
            w = self.w
            inbox = rfull if full else rlow
            self.flying = []
            for digit, dev in found:
                give = self.lo + digit * part
                at = self.used[full]
                self.used[full] += part
                if full:
                    out = acc.at[w, pl.ds(give, part)]
                else:
                    sbuf[w, pl.ds(give, part)] = acc[w, pl.ds(give, part)].astype(BF16)
                    out = sbuf.at[w, pl.ds(give, part)]
                copy = remote(out, inbox.at[w, at:at + part], w_s.at[w, self.sem], w_r.at[w, self.sem], dev)
                self.sem += 1
                copy.start()
                self.flying.append((copy, inbox, at))
            keep = self.lo + own * part
            self.done.append((keep, part, found))
            self.lo, self.length = keep, part

        def end(self):
            total = acc[self.w, pl.ds(self.lo, self.length)]
            for copy, inbox, at in self.flying:
                copy.wait()
                total = total + inbox[self.w, at:at + self.length].astype(F32)
            acc[self.w, pl.ds(self.lo, self.length)] = total

        def round(self):
            obuf[self.w, pl.ds(self.lo, self.length)] = acc[self.w, pl.ds(self.lo, self.length)].astype(BF16)

        def give(self, n):
            keep, part, found = self.done[n]
            self.flying = []
            for digit, dev in found:
                copy = remote(obuf.at[self.w, pl.ds(keep, part)], obuf.at[self.w, pl.ds(keep, part)],
                              w_s.at[self.w, self.sem], w_r.at[self.w, self.sem], dev)
                self.sem += 1
                copy.start()
                self.flying.append(copy)

        def given(self):
            for copy in self.flying:
                copy.wait()

        def advance(self):
            at, count = self.at, len(groups)
            self.at += 1
            if at < count:
                if at > 0:
                    self.end()
                self.begin(at)
            elif at == count:
                self.end()
                self.round()
                self.give(count - 1)
            elif at < 2 * count:
                self.given()
                self.give(2 * count - 1 - at)
            elif at == 2 * count:
                self.given()
                for n in range(9):
                    self.out[n] = obuf[self.w, n * per:(n + 1) * per].reshape(C, C)
                self.over = True

    barrier = pltpu.get_barrier_semaphore()

    @pl.loop(0, n_f)
    def _(df):
        @pl.loop(0, n_t)
        def _(dt):
            @pl.when(jnp.logical_or(df != f, dt != t))
            def _():
                pl.semaphore_signal(barrier, inc=1, device_id=where_to(dt, df), device_id_type=MESH)
    loads = [pltpu.make_async_copy(src, dst, in_s.at[n]) for n, (src, dst) in enumerate(
        ((fields_h, x.at[0]), (upstream_h, x.at[1]), (k1_h, k1), (k2_h, k2)))]
    for load in loads:
        load.start()
    fields, upstream, hidden, pre_grad = x.at[0], x.at[1], y.at[0], y.at[1]
    al[...] = jnp.zeros_like(al)
    tl[...] = jnp.zeros_like(tl)
    dl[...] = jnp.zeros_like(dl)
    loads[0].wait()
    loads[1].wait()
    stage(0, fields)
    stage(1, upstream)
    if blocks > 9 * per:
        for w in range(2):
            acc[w, 9 * per:blocks] = jnp.zeros((blocks - 9 * per, 16, C), F32)
    pl.semaphore_wait(barrier, n_t * n_f - 1)

    start(0, fields)
    start(1, upstream)
    loads[2].wait()
    loads[3].wait()
    await_arrivals(0, fields)
    forward_taps(0, fields, xf1)
    value, slope = gelu_parts(apply(xf1, k1, 0))
    unflat(value.astype(BF16), hidden)
    stage(2, hidden)
    start(2, hidden)
    await_arrivals(1, upstream)
    backward_taps(1, upstream, xb)
    cot = (apply(xb, k2, 1) * slope).astype(BF16)
    unflat(cot, pre_grad)
    stage(3, pre_grad)
    start(3, pre_grad)
    one, two = Sum(0, w1_o), Sum(1, w2_o)
    weight_terms(xf1, cot, 0)
    one.advance()
    one.advance()
    await_arrivals(2, hidden)
    forward_taps(2, hidden, xf2)
    weight_terms(xf2, flat(upstream), 1)
    two.advance()
    one.advance()
    two.advance()
    unflat(apply(xf2, k2, 0).astype(BF16), res_o)
    one.advance()
    two.advance()
    await_arrivals(3, pre_grad)
    backward_taps(3, pre_grad, xb)
    one.advance()
    two.advance()
    unflat(apply(xb, k1, 1).astype(BF16), fg_o)
    while not (one.over and two.over):
        one.advance()
        two.advance()
    await_sends(0, fields)
    await_sends(1, upstream)
    await_sends(2, hidden)
    await_sends(3, pre_grad)


def plan(n_t, n_f):
    tile_bits = [1 << i for i in range(n_t.bit_length() - 1)]
    face_bits = [1 << i for i in range(n_f.bit_length() - 1)]
    groups = [([("tile", tile_bits[0])], 1)]
    middle = [("face", s) for s in face_bits] + [("tile", s) for s in tile_bits[1:2]]
    rest = [("tile", s) for s in tile_bits[2:]]
    while middle:
        groups.append((middle[:2], 0))
        middle = middle[2:]
    while rest:
        groups.append((rest[:2], 0))
        rest = rest[2:]
    return groups


def run(fields, upstream, k1, k2, n_t, n_f):
    G, J, H, C = fields.shape
    S = H // 3
    E = J + 2
    M = G * J * H
    ranks = n_t * n_f
    blocks = -(-(9 * (C // 16)) // ranks) * ranks
    scale = 1.0 / (S * 12.0 ** 0.5)
    groups = plan(n_t, n_f)
    length, room, flights = blocks, [1, 1], 0
    for bits, full in groups:
        others = 2 ** len(bits) - 1
        length //= others + 1
        room[full] += length * others
        flights += others
    dma = pltpu.SemaphoreType.DMA
    vmem = pl.BlockSpec(memory_space=pltpu.VMEM)
    return pl.pallas_call(
        functools.partial(body, n_t, n_f, scale, groups),
        out_shape=(
            jax.ShapeDtypeStruct((G, J, H, C), BF16),
            jax.ShapeDtypeStruct((G, J, H, C), BF16),
            jax.ShapeDtypeStruct((9, C, C), BF16),
            jax.ShapeDtypeStruct((9, C, C), BF16),
        ),
        in_specs=[pl.BlockSpec(memory_space=pl.ANY)] * 2 + [pl.BlockSpec(memory_space=pltpu.HBM)] * 2,
        out_specs=[vmem] * 4,
        scratch_shapes=[
            pltpu.VMEM((2, G, J, H, C), BF16),
            pltpu.VMEM(k1.shape, BF16),
            pltpu.VMEM(k2.shape, BF16),
            pltpu.VMEM((2, G, J, H, C), BF16),
            pltpu.VMEM((4, 2, G, J, C), F32),
            pltpu.VMEM((4, G, H, C), BF16),
            pltpu.VMEM((4, G, H, C), BF16),
            pltpu.VMEM((4, G, E, C), F32),
            pltpu.VMEM((4, G, E, C), F32),
            pltpu.VMEM((4, n_t, G, E, C), F32),
            pltpu.VMEM((4, n_t, G, J, C), F32),
            pltpu.VMEM((4, n_t, G, J, C), F32),
            pltpu.VMEM((2, G, S + 16, C), F32),
            pltpu.VMEM((2, G, S + 16, C), F32),
            pltpu.VMEM((2, G, S + 32, C), F32),
            pltpu.VMEM((G, J + 2, H + 16, C), F32),
            pltpu.VMEM((9, M, C), F32),
            pltpu.VMEM((9, M, C), BF16),
            pltpu.VMEM((9, M, C), BF16),
            pltpu.VMEM((2, blocks, 16, C), F32),
            pltpu.VMEM((2, blocks, 16, C), BF16),
            pltpu.VMEM((2, room[0], 16, C), BF16),
            pltpu.VMEM((2, room[1], 16, C), F32),
            pltpu.VMEM((2, blocks, 16, C), BF16),
            dma((4, 6)), dma((4, 6)),
            dma((4, 2, n_t)), dma((4, 2)),
            dma((4, 2, n_t)), dma((4, 2)),
            dma((4, 2)), dma((4, 2, n_t)),
            dma((4, 2)), dma((4, 2, n_t)),
            dma((2, 2 * flights)), dma((2, 2 * flights)), dma((4,)),
        ],
        compiler_params=pltpu.CompilerParams(
            collective_id=0, has_side_effects=True, vmem_limit_bytes=24 * 1024 * 1024),
    )(fields, upstream, pltpu.with_memory_space_constraint(k1, pltpu.HBM), pltpu.with_memory_space_constraint(k2, pltpu.HBM))


def on_device(n_sub, n_t, n_f, fields, upstream, k1, k2):
    own = fields.shape[0]
    if n_sub > 1:
        fields = lax.all_gather(fields, "sub", axis=0, tiled=True)
        upstream = lax.all_gather(upstream, "sub", axis=0, tiled=True)
    res, fgrad, w1, w2 = run(
        fields.transpose(1, 2, 3, 0), upstream.transpose(1, 2, 3, 0), k1, k2, n_t, n_f)
    if n_sub > 1:
        at = lax.axis_index("sub") * own
        res = lax.dynamic_slice_in_dim(res, at, own, 3)
        fgrad = lax.dynamic_slice_in_dim(fgrad, at, own, 3)
        w1 = lax.dynamic_slice_in_dim(w1, at, own, 2)
        w2 = lax.dynamic_slice_in_dim(w2, at, own, 2)
    shape = (3, 3) + w1.shape[1:]
    return (res.transpose(3, 0, 1, 2), fgrad.transpose(3, 0, 1, 2), w1.astype(F32).reshape(shape), w2.astype(F32).reshape(shape))


def solution(mesh):
    placed = (P("sub", "face", "tile", "parts"), P("sub", "face", "tile", "parts"), P(), P())
    sizes = mesh.shape
    return jax.shard_map(
        functools.partial(on_device, sizes["sub"], sizes["tile"], sizes["face"]),
        mesh=mesh,
        in_specs=placed,
        out_specs=(
            P("sub", "face", "tile", "parts"),
            P("sub", "face", "tile", "parts"),
            P("parts", None, None, "sub"),
            P("parts", None, None, "sub"),
        ),
        check_vma=False,
    )
```

```python
import functools

import jax
import jax.numpy as jnp
from jax import lax
from jax.experimental import pallas as pl
from jax.experimental.pallas import tpu as pltpu
from jax.sharding import PartitionSpec as P

MESH = pl.DeviceIdType.MESH
F32 = jnp.float32
BF16 = jnp.bfloat16


def gelu_parts(v):
    root = 0.7978845608028654
    cube = 0.044715 * (v * v * v)
    th = jnp.tanh(root * (v + cube))
    value = v * (0.5 * (1.0 + th))
    slope = 0.5 * (1.0 + th) + 0.5 * v * (1.0 - th * th) * root * (1.0 + 0.134145 * (v * v))
    return value, slope


def product(a, b, da, db):
    return lax.dot_general(a, b, (((da,), (db,)), ((), ())), preferred_element_type=F32)


def body(n_t, n_f, scale, groups, fields_h, upstream_h, k1_h, k2_h, res_o, fg_o, w1_o, w2_o,
         x, k1, k2, y, rows, lh, rh, ap, bm, aps, tr, dr, tl, dl, al, pad, xb, xf1, xf2,
         acc, sbuf, rlow, rfull, obuf,
         col_s, col_r, a_s, a_r, b_s, b_r, t_s, t_r, d_s, d_r, w_s, w_r, in_s):
    _, G, J, H, C = x.shape
    S = H // 3
    E = J + 2
    t = lax.axis_index("tile")
    f = lax.axis_index("face")
    fn = lax.rem(f + 1, n_f)
    fp = lax.rem(f + n_f - 1, n_f)
    first = t == 0
    last = t == n_t - 1
    inner_left = jnp.logical_not(first)
    inner_right = jnp.logical_not(last)

    def where_to(tile, face):
        return {"tile": tile, "face": face}

    def remote(src, dst, s, r, dev):
        return pltpu.make_async_remote_copy(
            src_ref=src, dst_ref=dst, send_sem=s, recv_sem=r, device_id=dev, device_id_type=MESH)

    def copies(p, src):
        c0, cl = src.at[:, 0], src.at[:, J - 1]
        right = lambda: remote(cl, lh.at[p], col_s.at[p, 0], col_r.at[p, 0], where_to(jnp.minimum(t + 1, n_t - 1), f))
        left = lambda: remote(c0, rh.at[p], col_s.at[p, 1], col_r.at[p, 1], where_to(jnp.maximum(t - 1, 0), f))
        seam = []
        if G > 1:
            seam.append((first, lambda: remote(src.at[1:G, 0], rh.at[p, 0:G - 1], col_s.at[p, 2], col_r.at[p, 2], where_to(n_t - 1, f))))
            seam.append((last, lambda: remote(src.at[0:G - 1, J - 1], lh.at[p, 1:G], col_s.at[p, 3], col_r.at[p, 3], where_to(0, f))))
        seam.append((first, lambda: remote(src.at[0:1, 0], rh.at[p, G - 1:G], col_s.at[p, 4], col_r.at[p, 4], where_to(n_t - 1, fp))))
        seam.append((last, lambda: remote(src.at[G - 1:G, J - 1], lh.at[p, 0:1], col_s.at[p, 5], col_r.at[p, 5], where_to(0, fn))))
        a_own = lambda d: remote(aps.at[p, d, 1:G], ap.at[p, 0:G - 1], a_s.at[p, 0, d], a_r.at[p, 0], where_to(d, f))
        a_oth = lambda d: remote(aps.at[p, d, 0:1], ap.at[p, G - 1:G], a_s.at[p, 1, d], a_r.at[p, 1], where_to(d, fp))
        b_own = lambda d: remote(aps.at[p, d, 0:G - 1], bm.at[p, 1:G], b_s.at[p, 0, d], b_r.at[p, 0], where_to(d, f))
        b_oth = lambda d: remote(aps.at[p, d, G - 1:G], bm.at[p, 0:1], b_s.at[p, 1, d], b_r.at[p, 1], where_to(d, fn))
        t_own = lambda d: remote(rows.at[p, 0, 0:G - 1], tr.at[p, d, 1:G], t_s.at[p, 0], t_r.at[p, 0, d], where_to(0, f))
        t_oth = lambda d: remote(rows.at[p, 0, G - 1:G], tr.at[p, d, 0:1], t_s.at[p, 1], t_r.at[p, 1, d], where_to(0, fn))
        d_own = lambda d: remote(rows.at[p, 1, 1:G], dr.at[p, d, 0:G - 1], d_s.at[p, 0], d_r.at[p, 0, d], where_to(n_t - 1, f))
        d_oth = lambda d: remote(rows.at[p, 1, 0:1], dr.at[p, d, G - 1:G], d_s.at[p, 1], d_r.at[p, 1, d], where_to(n_t - 1, fp))
        return right, left, seam, a_own, a_oth, b_own, b_oth, t_own, t_oth, d_own, d_oth

    def stage(p, src):
        for q in range(G):
            for j in range(J):
                rows[p, 0, q, j:j + 1, :] = src[q, j, 0:16].astype(F32)[0:1]
                rows[p, 1, q, j:j + 1, :] = src[q, j, H - 16:H].astype(F32)[15:16]

        @pl.when(first)
        def _():
            more = 16 * (p % 2)
            for q in range(G):
                al[p % 2, q, 16:16 + S + more, :] = src[q, 0, 0:S + more].astype(F32)
            for d in range(n_t):
                aps[p, d] = al[p % 2, :, 15 + d * J:15 + d * J + E, :]

        @pl.when(last)
        def _():
            more = 16 * (p % 2)
            for q in range(G):
                al[p % 2, q, 16 - more:16 + S, :] = src[q, J - 1, 2 * S - more:H].astype(F32)
            for d in range(n_t):
                aps[p, d] = al[p % 2, :, 15 + d * J:15 + d * J + E, :]

    def start(p, src):
        right, left, seam, a_own, a_oth, b_own, b_oth, t_own, t_oth, d_own, d_oth = copies(p, src)
        t_oth(t).start()
        d_oth(t).start()
        if G > 1:
            @pl.when(inner_left)
            def _():
                t_own(t).start()

            @pl.when(inner_right)
            def _():
                d_own(t).start()
        for cond, make in seam:
            @pl.when(cond)
            def _(make=make):
                make().start()

        @pl.when(first)
        def _():
            @pl.loop(0, n_t)
            def _(d):
                a_oth(n_t - 1 - d).start()
            if G > 1:
                @pl.loop(1, n_t)
                def _(d):
                    a_own(n_t - d).start()
                ap[p, 0:G - 1] = aps[p, 0, 1:G]
                tr[p, 0, 1:G] = rows[p, 0, 0:G - 1]

        @pl.when(last)
        def _():
            @pl.loop(0, n_t)
            def _(d):
                b_oth(d).start()
            if G > 1:
                @pl.loop(0, n_t - 1)
                def _(d):
                    b_own(d).start()
                bm[p, 1:G] = aps[p, n_t - 1, 0:G - 1]
                dr[p, n_t - 1, 0:G - 1] = rows[p, 1, 1:G]

        @pl.when(inner_right)
        def _():
            right().start()

        @pl.when(inner_left)
        def _():
            left().start()

    def await_arrivals(p, src):
        right, left, seam, a_own, a_oth, b_own, b_oth, t_own, t_oth, d_own, d_oth = copies(p, src)

        @pl.when(inner_left)
        def _():
            right().wait_recv()
            if G > 1:
                a_own(0).wait_recv()

        @pl.when(inner_right)
        def _():
            left().wait_recv()
            if G > 1:
                b_own(0).wait_recv()

        for cond, make in seam:
            @pl.when(last if cond is first else first)
            def _(make=make):
                make().wait_recv()

        a_oth(0).wait_recv()
        b_oth(0).wait_recv()

        @pl.when(first)
        def _():
            if G > 1:
                @pl.loop(1, n_t)
                def _(d):
                    t_own(d).wait_recv()

            @pl.loop(0, n_t)
            def _(d):
                t_oth(d).wait_recv()
            for d in range(n_t):
                tl[p % 2, :, 8 + d * J:8 + (d + 1) * J, :] = tr[p, d]

        @pl.when(last)
        def _():
            if G > 1:
                @pl.loop(0, n_t - 1)
                def _(d):
                    d_own(d).wait_recv()

            @pl.loop(0, n_t)
            def _(d):
                d_oth(d).wait_recv()
            for d in range(n_t):
                dl[p % 2, :, 8 + d * J:8 + (d + 1) * J, :] = dr[p, d]

    def await_sends(p, src):
        right, left, seam, a_own, a_oth, b_own, b_oth, t_own, t_oth, d_own, d_oth = copies(p, src)

        @pl.when(inner_right)
        def _():
            right().wait_send()
            if G > 1:
                d_own(t).wait_send()

        @pl.when(inner_left)
        def _():
            left().wait_send()
            if G > 1:
                t_own(t).wait_send()

        for cond, make in seam:
            @pl.when(cond)
            def _(make=make):
                make().wait_send()
        t_oth(t).wait_send()
        d_oth(t).wait_send()

        @pl.when(first)
        def _():
            if G > 1:
                @pl.loop(1, n_t)
                def _(d):
                    a_own(d).wait_send()

            @pl.loop(0, n_t)
            def _(d):
                a_oth(d).wait_send()

        @pl.when(last)
        def _():
            if G > 1:
                @pl.loop(0, n_t - 1)
                def _(d):
                    b_own(d).wait_send()

            @pl.loop(0, n_t)
            def _(d):
                b_oth(d).wait_send()

    def fill_columns(src):
        for q in range(G):
            for j in range(J):
                pad[q, 1 + j, 8:8 + H, :] = src[q, j].astype(F32)

    def forward_taps(p, src, out):
        fill_columns(src)
        for q in range(G):
            @pl.when(inner_left)
            def _():
                pad[q, 0, 8:8 + H, :] = lh[p, q].astype(F32)

            @pl.when(first)
            def _():
                pad[q, 0, 8:8 + S, :] = tl[0, q, 8:8 + S, :]
                pad[q, 0, 8 + S:8 + H, :] = lh[p, q, 0:2 * S].astype(F32)

            @pl.when(inner_right)
            def _():
                pad[q, J + 1, 8:8 + H, :] = rh[p, q].astype(F32)

            @pl.when(last)
            def _():
                pad[q, J + 1, 8:8 + 2 * S, :] = rh[p, q, S:H].astype(F32)
                pad[q, J + 1, 8 + 2 * S:8 + H, :] = dl[0, q, 8:8 + S, :]
            for j in range(E):
                pad[q, j, 7:8, :] = ap[p, q, j:j + 1]
                pad[q, j, 8 + H:9 + H, :] = bm[p, q, j:j + 1]
        for a in range(3):
            for b in range(3):
                for q in range(G):
                    for j in range(J):
                        m = (q * J + j) * H
                        out[3 * a + b, m:m + H, :] = pad[q, j + a, 7 + b:7 + b + H, :].astype(BF16)

    def backward_taps(p, src, out):
        fill_columns(src)
        for q in range(G):
            @pl.when(inner_left)
            def _():
                pad[q, 0, 8:8 + H, :] = lh[p, q].astype(F32)

            @pl.when(first)
            def _():
                pad[q, 0, :, :] = jnp.zeros((H + 16, C), F32)

            @pl.when(inner_right)
            def _():
                pad[q, J + 1, 8:8 + H, :] = rh[p, q].astype(F32)

            @pl.when(last)
            def _():
                pad[q, J + 1, :, :] = jnp.zeros((H + 16, C), F32)
            for j in range(E):
                pad[q, j, 7:8, :] = jnp.zeros((1, C), F32)
                pad[q, j, 8 + H:9 + H, :] = jnp.zeros((1, C), F32)
        for a in range(3):
            for b in range(3):
                for q in range(G):
                    for j in range(J):
                        m = (q * J + j) * H
                        out[3 * a + b, m:m + H, :] = pad[q, j - a + 2, 9 - b:9 - b + H, :]
        for q in range(G):
            top = ap[p, q]
            low = bm[p, q]
            for b in range(3):
                for j in range(J):
                    m = (q * J + j) * H
                    out[b, m:m + 1, :] += top[j + 2 - b:j + 3 - b]
                    out[6 + b, m + H - 1:m + H, :] += low[j + 2 - b:j + 3 - b]

        @pl.when(last)
        def _():
            for q in range(G):
                m = (q * J + J - 1) * H
                pad[q, J + 1, 8:8 + H, :] = rh[p, q].astype(F32)
                for e in range(3):
                    out[e, m:m + 2 * S, :] += pad[q, J + 1, 8 + S + 1 - e:8 + H + 1 - e, :]
                    out[3 * e + 2, m + 2 * S:m + H, :] += dl[1, q, 9 - e:9 - e + S, :]

        @pl.when(first)
        def _():
            for q in range(G):
                m = q * J * H
                pad[q, 0, 8:8 + H, :] = lh[p, q].astype(F32)
                for e in range(3):
                    out[3 * e, m:m + S, :] += tl[1, q, 9 - e:9 - e + S, :]
                    out[6 + e, m + S:m + H, :] += pad[q, 0, 9 - e:9 - e + 2 * S, :]

    def apply(taps, k, dim):
        total = product(taps[0].astype(BF16), k[0, 0], 1, dim)
        for n in range(1, 9):
            total = total + product(taps[n].astype(BF16), k[n // 3, n % 3], 1, dim)
        return total

    def flat(src):
        return jnp.concatenate([src[q, j] for q in range(G) for j in range(J)], axis=0)

    def unflat(value, dst):
        for q in range(G):
            for j in range(J):
                m = (q * J + j) * H
                dst[q, j] = value[m:m + H]

    per = C // 16
    blocks = acc.shape[1]

    def weight_terms(taps, cot, w):
        for n in range(9):
            term = product(taps[n], cot, 0, 0) * scale
            acc[w, n * per:(n + 1) * per] = term.reshape(per, 16, C)

    class Sum:
        def __init__(self, w, out):
            self.out, self.at, self.over = out, 0, False
            self.w, self.lo, self.length, self.done = w, 0, blocks, []
            self.used = [0, 0]
            self.sem = 0

        def members(self, bits):
            mine, place = [], 0
            for axis, s in bits:
                mine.append(lax.rem((t if axis == "tile" else f) // s, 2))
            found = []
            for k in range(1, 2 ** len(bits)):
                tile, face, digit = t, f, 0
                for pos, (axis, s) in enumerate(bits):
                    bit = mine[pos]
                    if (k >> pos) & 1:
                        if axis == "tile":
                            tile = tile + (1 - 2 * bit) * s
                        else:
                            face = face + (1 - 2 * bit) * s
                        bit = 1 - bit
                    digit = digit + bit * (1 << pos)
                found.append((digit, where_to(tile, face)))
            own = 0
            for pos, bit in enumerate(mine):
                own = own + bit * (1 << pos)
            return own, found

        def begin(self, n):
            bits, full = groups[n]
            own, found = self.members(bits)
            part = self.length // (len(found) + 1)
            w = self.w
            inbox = rfull if full else rlow
            self.flying = []
            for digit, dev in found:
                give = self.lo + digit * part
                at = self.used[full]
                self.used[full] += part
                if full:
                    out = acc.at[w, pl.ds(give, part)]
                else:
                    sbuf[w, pl.ds(give, part)] = acc[w, pl.ds(give, part)].astype(BF16)
                    out = sbuf.at[w, pl.ds(give, part)]
                copy = remote(out, inbox.at[w, at:at + part], w_s.at[w, self.sem], w_r.at[w, self.sem], dev)
                self.sem += 1
                copy.start()
                self.flying.append((copy, inbox, at))
            keep = self.lo + own * part
            self.done.append((keep, part, found))
            self.lo, self.length = keep, part

        def end(self):
            total = acc[self.w, pl.ds(self.lo, self.length)]
            for copy, inbox, at in self.flying:
                copy.wait()
                total = total + inbox[self.w, at:at + self.length].astype(F32)
            acc[self.w, pl.ds(self.lo, self.length)] = total

        def round(self):
            obuf[self.w, pl.ds(self.lo, self.length)] = acc[self.w, pl.ds(self.lo, self.length)].astype(BF16)

        def give(self, n):
            keep, part, found = self.done[n]
            self.flying = []
            for digit, dev in found:
                copy = remote(obuf.at[self.w, pl.ds(keep, part)], obuf.at[self.w, pl.ds(keep, part)],
                              w_s.at[self.w, self.sem], w_r.at[self.w, self.sem], dev)
                self.sem += 1
                copy.start()
                self.flying.append(copy)

        def given(self):
            for copy in self.flying:
                copy.wait()

        def advance(self):
            at, count = self.at, len(groups)
            self.at += 1
            if at < count:
                if at > 0:
                    self.end()
                self.begin(at)
            elif at == count:
                self.end()
                self.round()
                self.give(count - 1)
            elif at < 2 * count:
                self.given()
                self.give(2 * count - 1 - at)
            elif at == 2 * count:
                self.given()
                for n in range(9):
                    self.out[n] = obuf[self.w, n * per:(n + 1) * per].reshape(C, C)
                self.over = True

    barrier = pltpu.get_barrier_semaphore()

    @pl.loop(0, n_f)
    def _(df):
        @pl.loop(0, n_t)
        def _(dt):
            @pl.when(jnp.logical_or(df != f, dt != t))
            def _():
                pl.semaphore_signal(barrier, inc=1, device_id=where_to(dt, df), device_id_type=MESH)
    loads = [pltpu.make_async_copy(src, dst, in_s.at[n]) for n, (src, dst) in enumerate(
        ((fields_h, x.at[0]), (upstream_h, x.at[1]), (k1_h, k1), (k2_h, k2)))]
    for load in loads:
        load.start()
    fields, upstream, hidden, pre_grad = x.at[0], x.at[1], y.at[0], y.at[1]
    al[...] = jnp.zeros_like(al)
    tl[...] = jnp.zeros_like(tl)
    dl[...] = jnp.zeros_like(dl)
    loads[0].wait()
    loads[1].wait()
    stage(0, fields)
    if blocks > 9 * per:
        for w in range(2):
            acc[w, 9 * per:blocks] = jnp.zeros((blocks - 9 * per, 16, C), F32)
    pl.semaphore_wait(barrier, n_t * n_f - 1)

    start(0, fields)
    stage(1, upstream)
    start(1, upstream)
    loads[2].wait()
    loads[3].wait()
    await_arrivals(0, fields)
    forward_taps(0, fields, xf1)
    value, slope = gelu_parts(apply(xf1, k1, 0))
    unflat(value.astype(BF16), hidden)
    stage(2, hidden)
    start(2, hidden)
    await_arrivals(1, upstream)
    backward_taps(1, upstream, xb)
    cot = (apply(xb, k2, 1) * slope).astype(BF16)
    unflat(cot, pre_grad)
    stage(3, pre_grad)
    start(3, pre_grad)
    one, two = Sum(0, w1_o), Sum(1, w2_o)
    cells = flat(hidden)
    for n in range(9):
        term = product(cells, xb[n].astype(BF16), 0, 0) * scale
        acc[1, n * per:(n + 1) * per] = term.reshape(per, 16, C)
    two.advance()
    weight_terms(xf1, cot, 0)
    one.advance()
    two.advance()
    one.advance()
    await_arrivals(2, hidden)
    forward_taps(2, hidden, xf2)
    unflat(apply(xf2, k2, 0).astype(BF16), res_o)
    two.advance()
    one.advance()
    await_arrivals(3, pre_grad)
    backward_taps(3, pre_grad, xb)
    unflat(apply(xb, k1, 1).astype(BF16), fg_o)
    while not (one.over and two.over):
        one.advance()
        two.advance()
    await_sends(0, fields)
    await_sends(1, upstream)
    await_sends(2, hidden)
    await_sends(3, pre_grad)


def plan(n_t, n_f):
    tile_bits = [1 << i for i in range(n_t.bit_length() - 1)]
    face_bits = [1 << i for i in range(n_f.bit_length() - 1)]
    groups = [([("tile", tile_bits[0])], 1)]
    middle = [("face", s) for s in face_bits] + [("tile", s) for s in tile_bits[1:2]]
    rest = [("tile", s) for s in tile_bits[2:]]
    while middle:
        groups.append((middle[:2], 0))
        middle = middle[2:]
    while rest:
        groups.append((rest[:2], 0))
        rest = rest[2:]
    return groups


def run(fields, upstream, k1, k2, n_t, n_f):
    G, J, H, C = fields.shape
    S = H // 3
    E = J + 2
    M = G * J * H
    ranks = n_t * n_f
    blocks = -(-(9 * (C // 16)) // ranks) * ranks
    scale = 1.0 / (S * 12.0 ** 0.5)
    groups = plan(n_t, n_f)
    length, room, flights = blocks, [1, 1], 0
    for bits, full in groups:
        others = 2 ** len(bits) - 1
        length //= others + 1
        room[full] += length * others
        flights += others
    dma = pltpu.SemaphoreType.DMA
    vmem = pl.BlockSpec(memory_space=pltpu.VMEM)
    return pl.pallas_call(
        functools.partial(body, n_t, n_f, scale, groups),
        out_shape=(
            jax.ShapeDtypeStruct((G, J, H, C), BF16),
            jax.ShapeDtypeStruct((G, J, H, C), BF16),
            jax.ShapeDtypeStruct((9, C, C), BF16),
            jax.ShapeDtypeStruct((9, C, C), BF16),
        ),
        in_specs=[pl.BlockSpec(memory_space=pl.ANY)] * 2 + [pl.BlockSpec(memory_space=pltpu.HBM)] * 2,
        out_specs=[vmem] * 4,
        scratch_shapes=[
            pltpu.VMEM((2, G, J, H, C), BF16),
            pltpu.VMEM(k1.shape, BF16),
            pltpu.VMEM(k2.shape, BF16),
            pltpu.VMEM((2, G, J, H, C), BF16),
            pltpu.VMEM((4, 2, G, J, C), F32),
            pltpu.VMEM((4, G, H, C), BF16),
            pltpu.VMEM((4, G, H, C), BF16),
            pltpu.VMEM((4, G, E, C), F32),
            pltpu.VMEM((4, G, E, C), F32),
            pltpu.VMEM((4, n_t, G, E, C), F32),
            pltpu.VMEM((4, n_t, G, J, C), F32),
            pltpu.VMEM((4, n_t, G, J, C), F32),
            pltpu.VMEM((2, G, S + 16, C), F32),
            pltpu.VMEM((2, G, S + 16, C), F32),
            pltpu.VMEM((2, G, S + 32, C), F32),
            pltpu.VMEM((G, J + 2, H + 16, C), F32),
            pltpu.VMEM((9, M, C), F32),
            pltpu.VMEM((9, M, C), BF16),
            pltpu.VMEM((9, M, C), BF16),
            pltpu.VMEM((2, blocks, 16, C), F32),
            pltpu.VMEM((2, blocks, 16, C), BF16),
            pltpu.VMEM((2, room[0], 16, C), BF16),
            pltpu.VMEM((2, room[1], 16, C), F32),
            pltpu.VMEM((2, blocks, 16, C), BF16),
            dma((4, 6)), dma((4, 6)),
            dma((4, 2, n_t)), dma((4, 2)),
            dma((4, 2, n_t)), dma((4, 2)),
            dma((4, 2)), dma((4, 2, n_t)),
            dma((4, 2)), dma((4, 2, n_t)),
            dma((2, 2 * flights)), dma((2, 2 * flights)), dma((4,)),
        ],
        compiler_params=pltpu.CompilerParams(
            collective_id=0, has_side_effects=True, vmem_limit_bytes=24 * 1024 * 1024),
    )(fields, upstream, pltpu.with_memory_space_constraint(k1, pltpu.HBM), pltpu.with_memory_space_constraint(k2, pltpu.HBM))


def on_device(n_sub, n_t, n_f, fields, upstream, k1, k2):
    own = fields.shape[0]
    if n_sub > 1:
        fields = lax.all_gather(fields, "sub", axis=0, tiled=True)
        upstream = lax.all_gather(upstream, "sub", axis=0, tiled=True)
    res, fgrad, w1, w2 = run(
        fields.transpose(1, 2, 3, 0), upstream.transpose(1, 2, 3, 0), k1, k2, n_t, n_f)
    if n_sub > 1:
        at = lax.axis_index("sub") * own
        res = lax.dynamic_slice_in_dim(res, at, own, 3)
        fgrad = lax.dynamic_slice_in_dim(fgrad, at, own, 3)
        w1 = lax.dynamic_slice_in_dim(w1, at, own, 2)
        w2 = lax.dynamic_slice_in_dim(w2, at, own, 2)
    shape = (3, 3) + w1.shape[1:]
    return (res.transpose(3, 0, 1, 2), fgrad.transpose(3, 0, 1, 2), w1.astype(F32).reshape(shape), w2.astype(F32).reshape(shape))


def solution(mesh):
    placed = (P("sub", "face", "tile", "parts"), P("sub", "face", "tile", "parts"), P(), P())
    sizes = mesh.shape
    return jax.shard_map(
        functools.partial(on_device, sizes["sub"], sizes["tile"], sizes["face"]),
        mesh=mesh,
        in_specs=placed,
        out_specs=(
            P("sub", "face", "tile", "parts"),
            P("sub", "face", "tile", "parts"),
            P("parts", None, None, "sub"),
            P("parts", None, None, "sub"),
        ),
        check_vma=False,
    )
```
